32 devices in a mesh: lat: 8 (over y, x, core), lon: 4 (over z).
Axes of the slice: x: 2, y: 2, z: 4, core: 2. Of those that a mesh axis runs over, the one named last changes fastest.
Arguments:
- prediction_deviation: bfloat16 [16, 256, 128, 80], P(None, 'lat', 'lon'), may hold values from -6 to 6
- humid_energy_misfit: float32 [16, 256, 128], P(None, 'lat', 'lon'), may hold values from -0.6 to 0.6
- sensor_space_deviation: bfloat16 [8, 4, 80, 1024], P('lat', 'lon'), may hold values from -6 to 6
- scaled_departure: float32 [8, 4, 1024], P('lat', 'lon'), may hold values from -6 to 6
- datum_location: int32 [8, 4, 2, 1024], P('lat', 'lon'), may hold values from 0 to 31, as said below
- taper_category: int32 [8, 4, 1024], P('lat', 'lon'), may hold values from 0 to 3
- datum_patch_codes: int32 [8, 4, 4, 1024], P('lat', 'lon'), may hold values from -1 to 8, as said below
- active_datum_tally: int32 [8, 4], P('lat', 'lon'), may hold values from 128 to 1024, as said below
Outputs:
- impact: float32 [8, 4, 1024], P('lat', 'lon')
The draws below stay inside these ranges and needn't reach their ends.
Inputs may be any that keep to these rules, and one draw needn't show every extreme that they name: `datum_location`: row and column of the observation's cell, each from 0 to 31. `datum_patch_codes`: codes are 3 (dr + 1) + (ds + 1) for a tile offset (dr, ds) from the owner, or -1 for an empty entry. Entry 0 is always 4, the owner; the named codes of a slot are distinct and never name a tile beyond the first or last tile row. At least 128 live slots on every tile, and 1024 on some tile in every draw; slots from active_datum_tally on carry no observation.
All inputs are finite; a program needn't handle non-finite values.
Results may differ from the reference program's by a relative error of at most 0.0055.
Values may be sent and summed in bfloat16 or wider, within the bound.
A program may use at most 64 MiB of HBM per device.

```python
import jax
import jax.numpy as jnp
from jax import lax

RUN_TOTAL = 80
STRATA_TOTAL = 16
TW = 32
OBS_DEV = 1024
LAT_TILES = 8
LON_TILES = 4
NORTH_SOUTH_SPAN = 256
EAST_WEST_SPAN = 128


def obs_geometry(key):
    base = jax.random.fold_in(key, 7)
    first, second, third = jax.random.split(base, 3)
    array_shape = (LAT_TILES, LON_TILES, OBS_DEV)
    rows_drawn = jax.random.randint(first, array_shape, 0, TW, dtype=jnp.int32)
    cols_drawn = jax.random.randint(second, array_shape, 0, TW, dtype=jnp.int32)
    classes = jax.random.randint(third, array_shape, 0, 4, dtype=jnp.int32)
    return (rows_drawn, cols_drawn, classes)


def draw_humid_energy_misfit(key, part):
    base = jax.random.fold_in(key, 23)
    first = jax.random.fold_in(base, 0)
    array_shape = (STRATA_TOTAL, NORTH_SOUTH_SPAN, EAST_WEST_SPAN)
    drawn = 0.1 * jnp.clip(jax.random.normal(first, array_shape, jnp.float32), -6.0, 6.0)
    return drawn.astype(jnp.float32)


def draw_scaled_departure(key, part):
    base = jax.random.fold_in(key, 29)
    first = jax.random.fold_in(base, 0)
    array_shape = (LAT_TILES, LON_TILES, OBS_DEV)
    drawn = jnp.clip(jax.random.normal(first, array_shape, jnp.float32), -6.0, 6.0)
    return drawn.astype(jnp.float32)


def draw_datum_location(key, part):
    rows_drawn, cols_drawn, classes = obs_geometry(key)
    return jnp.stack([rows_drawn, cols_drawn], axis=2).astype(jnp.int32)


def draw_taper_category(key, part):
    rows_drawn, cols_drawn, classes = obs_geometry(key)
    return classes


def draw_datum_patch_codes(key, part):
    rows_drawn, cols_drawn, classes = obs_geometry(key)
    skipping = jax.random.randint(jax.random.fold_in(key, 13), rows_drawn.shape, 0, 8, dtype=jnp.int32)
    reach_cells = TW * (1 + classes)
    tile_rows = jnp.arange(LAT_TILES, dtype=jnp.int32)[:, None, None]
    upward = (8 * (rows_drawn + 1) < reach_cells) & (tile_rows > 0)
    downward = (8 * (TW - rows_drawn) < reach_cells) & (tile_rows < LAT_TILES - 1)
    leftward = 8 * (cols_drawn + 1) < reach_cells
    rightward = 8 * (TW - cols_drawn) < reach_cells
    row_step = jnp.where(upward, -1, jnp.where(downward, 1, 0))
    col_step = jnp.where(leftward, -1, jnp.where(rightward, 1, 0))
    has_row = upward | downward
    has_col = leftward | rightward
    own_code = jnp.full(rows_drawn.shape, 4, jnp.int32)
    row_code = jnp.where(has_row & (skipping != 1), 3 * (row_step + 1) + 1, -1)
    col_code = jnp.where(has_col & (skipping != 2), 3 + col_step + 1, -1)
    corner_code = jnp.where(has_row & has_col & (skipping != 0), 3 * (row_step + 1) + col_step + 1, -1)
    return jnp.stack([own_code, row_code, col_code, corner_code], axis=2).astype(jnp.int32)


def draw_active_datum_tally(key, part):
    base = jax.random.fold_in(key, 11)
    first, second, third, fourth = jax.random.split(base, 4)
    array_shape = (LAT_TILES, LON_TILES)
    drawn = jax.random.randint(first, array_shape, OBS_DEV // 8, OBS_DEV // 2 + 1, dtype=jnp.int32)
    crowded = jax.random.randint(second, array_shape, 0, 4, dtype=jnp.int32) == 0
    dense = OBS_DEV - jax.random.randint(third, array_shape, 0, OBS_DEV // 8, dtype=jnp.int32)
    counts = jnp.where(crowded, dense, drawn)
    chosen = jax.random.randint(fourth, (), 0, LAT_TILES * LON_TILES, dtype=jnp.int32)
    flat_index = jnp.arange(LAT_TILES * LON_TILES, dtype=jnp.int32).reshape(array_shape)
    return jnp.where(flat_index == chosen, OBS_DEV, counts).astype(jnp.int32)


def steps_of(key, extent, cuts, smallest, top_value):
    factor_of, own = 1.0, jax.random.fold_in(key, 6)
    for dim, shards_of in cuts:
        draws = jnp.exp(jax.random.uniform(jax.random.fold_in(own, dim), (shards_of,), jnp.float32, smallest / len(cuts), top_value / len(cuts)))
        factor_of = factor_of * jnp.repeat(draws, extent[dim] // shards_of).reshape([-1 if axis == dim else 1 for axis in range(len(extent))])
    return factor_of


def noise(own_key, dims, spread, bound, pieces=(), kind=jnp.bfloat16):
    factor_of = steps_of(own_key, dims, pieces, -0.22, 0.18) if pieces else 1.0
    array = jax.random.normal(own_key, dims, jnp.float32) * spread * factor_of
    return jnp.minimum(jnp.maximum(array, -bound), bound).astype(kind)


def setup_inputs(seed: int = 0) -> dict:
    key_list = jax.random.split(jax.random.key(seed), 9)
    prediction_deviation = noise(key_list[0], (STRATA_TOTAL, NORTH_SOUTH_SPAN, EAST_WEST_SPAN, RUN_TOTAL), 1.0, 6.0, ((1, 8), (2, 4)))
    humid_energy_misfit = draw_humid_energy_misfit(jax.random.fold_in(key_list[8], 71), 0)
    sensor_space_deviation = noise(key_list[2], (LAT_TILES, LON_TILES, RUN_TOTAL, OBS_DEV), 1.0, 6.0, ((0, 8), (1, 4)))
    scaled_departure = draw_scaled_departure(jax.random.fold_in(key_list[8], 71), 0)
    datum_location = draw_datum_location(jax.random.fold_in(key_list[8], 71), 0)
    taper_category = draw_taper_category(jax.random.fold_in(key_list[8], 71), 0)
    datum_patch_codes = draw_datum_patch_codes(jax.random.fold_in(key_list[8], 71), 0)
    active_datum_tally = draw_active_datum_tally(jax.random.fold_in(key_list[8], 71), 0)
    return dict(prediction_deviation=prediction_deviation, humid_energy_misfit=humid_energy_misfit, sensor_space_deviation=sensor_space_deviation, scaled_departure=scaled_departure, datum_location=datum_location, taper_category=taper_category, datum_patch_codes=datum_patch_codes, active_datum_tally=active_datum_tally)


def taper_weights(obs_row, obs_col, obs_class, cell_rows, cell_cols, allowed, patch_span_points):
    radius = patch_span_points * (1.0 + obs_class) * 0.125
    radius_sq = (radius * radius)[:, None]
    distance = (cell_rows[None, :] - obs_row[:, None]) ** 2 + (cell_cols[None, :] - obs_col[:, None]) ** 2
    fraction = 1.0 - distance / radius_sq
    return jnp.where(allowed & (distance < radius_sq), fraction * fraction, 0.0).astype(jnp.bfloat16)


def tile_offset(shifted, patch_span_points):
    return (shifted >= patch_span_points).astype(jnp.int32) - (shifted < 0).astype(jnp.int32)


def reference(prediction_deviation, humid_energy_misfit, sensor_space_deviation, scaled_departure, datum_location, taper_category, datum_patch_codes, active_datum_tally):
    patch_span_points = TW
    margin = TW // 2
    window_width = 2 * TW

    def add_level(stratum_index, summed):
        altitude_stratum = lax.dynamic_index_in_dim(prediction_deviation, stratum_index, 0, keepdims=False).astype(jnp.float32)
        weight = lax.dynamic_index_in_dim(humid_energy_misfit, stratum_index, 0, keepdims=False)
        return summed + altitude_stratum * weight[..., None]

    summed = lax.fori_loop(0, STRATA_TOTAL, add_level, jnp.zeros((NORTH_SOUTH_SPAN, EAST_WEST_SPAN, RUN_TOTAL), jnp.float32))
    projected = summed.astype(jnp.bfloat16)
    padded = jnp.pad(projected, ((margin, margin), (0, 0), (0, 0)))
    padded = jnp.concatenate([padded[:, EAST_WEST_SPAN - margin:], padded, padded[:, :margin]], axis=1)

    offsets = jnp.arange(window_width, dtype=jnp.int32) - margin
    rel_rows = jnp.repeat(offsets, window_width)
    rel_cols = jnp.tile(offsets, window_width)
    tile_code = 3 * (tile_offset(rel_rows, patch_span_points) + 1) + tile_offset(rel_cols, patch_span_points) + 1
    cell_rows = rel_rows.astype(jnp.float32)
    cell_cols = rel_cols.astype(jnp.float32)

    tile_total = LAT_TILES * LON_TILES
    anomaly_all = sensor_space_deviation.reshape(tile_total, RUN_TOTAL, OBS_DEV)
    innovation_all = scaled_departure.reshape(tile_total, OBS_DEV)
    place_all = datum_location.reshape(tile_total, 2, OBS_DEV)
    class_all = taper_category.reshape(tile_total, OBS_DEV)
    cover_all = datum_patch_codes.reshape(tile_total, 4, OBS_DEV)
    count_all = active_datum_tally.reshape(tile_total)

    def one_tile(tile_index):
        tile_row = tile_index // LON_TILES
        tile_col = tile_index % LON_TILES
        window = lax.dynamic_slice(padded, (tile_row * patch_span_points, tile_col * patch_span_points, jnp.int32(0)),
                                   (window_width, window_width, RUN_TOTAL)).reshape(window_width * window_width, RUN_TOTAL)
        anomaly = lax.dynamic_index_in_dim(anomaly_all, tile_index, 0, keepdims=False)
        scaled = lax.dynamic_index_in_dim(innovation_all, tile_index, 0, keepdims=False)
        position = lax.dynamic_index_in_dim(place_all, tile_index, 0, keepdims=False).astype(jnp.float32)
        taper_size = lax.dynamic_index_in_dim(class_all, tile_index, 0, keepdims=False).astype(jnp.float32)
        cover_codes = lax.dynamic_index_in_dim(cover_all, tile_index, 0, keepdims=False)
        count_here = lax.dynamic_index_in_dim(count_all, tile_index, 0, keepdims=False)
        allowed = jnp.any(cover_codes[:, :, None] == tile_code[None, None, :], axis=0)
        weights = taper_weights(position[0], position[1], taper_size, cell_rows, cell_cols, allowed, patch_span_points)
        projection = jnp.dot(weights.astype(jnp.float32), window.astype(jnp.float32),
                             precision=lax.Precision.HIGHEST)
        summed_here = jnp.sum(projection * anomaly.T.astype(jnp.float32), axis=1)
        live_slots = (jnp.arange(OBS_DEV, dtype=jnp.int32) < count_here).astype(jnp.float32)
        return scaled * summed_here / (RUN_TOTAL - 1) * live_slots

    impacts = lax.map(one_tile, jnp.arange(tile_total, dtype=jnp.int32))
    return impacts.reshape(LAT_TILES, LON_TILES, OBS_DEV)
```

```python
import functools

import jax
import jax.numpy as jnp
from jax import lax
from jax.experimental import pallas as pl
from jax.experimental.pallas import tpu as pltpu
from jax.sharding import PartitionSpec as P

MESH = pl.DeviceIdType.MESH
HALF_CHUNKS = 2


def kernel(
    nlat, nlon,
    dev_hbm, mis_hbm, sens_hbm, scaled_hbm, loc_hbm, cat_hbm, codes_hbm, tally_hbm,
    out_ref,
    dev, mis, sens, scaled, loc, cat, codes,
    split, cells, own, halo, bound, taper, acc,
    in_sem, dev_sem, send_sem, recv_sem,
):
    levels, tile, _, members = dev.shape
    half = tile // 2
    slots = sens.shape[1]
    p = lax.axis_index("lat")
    q = lax.axis_index("lon")
    left = lax.rem(q + nlon - 1, nlon)
    right = lax.rem(q + 1, nlon)
    has_up = p > 0
    has_down = p < nlat - 1

    first = lax.rem(p, 2)
    halves = (first, 1 - first)
    present = [jnp.where(yh == 1, nlat - 1 - p, p) > 0 for yh in halves]
    rows_per = half // HALF_CHUNKS
    small = [
        pltpu.make_async_copy(src, dst, in_sem.at[i])
        for i, (src, dst) in enumerate(
            [(mis_hbm, mis), (loc_hbm, loc), (cat_hbm, cat), (codes_hbm, codes),
             (sens_hbm, sens), (scaled_hbm, scaled)]
        )
    ]
    reads = []
    for yh in halves:
        for c in range(HALF_CHUNKS):
            rows = pl.ds(yh * half + c * rows_per, rows_per)
            reads.append(
                pltpu.make_async_copy(dev_hbm.at[:, rows], dev.at[:, rows], dev_sem.at[len(reads)])
            )
    small[0].start()
    reads[0].start()
    for copy in small[1:4]:
        copy.start()
    for copy in reads[1:]:
        copy.start()
    for copy in small[4:]:
        copy.start()

    barrier = pltpu.get_barrier_semaphore()

    def greet(row):
        for col in (left, q, right):
            pl.semaphore_signal(barrier, inc=1, device_id=(row, col), device_id_type=MESH)

    for col in (left, right):
        pl.semaphore_signal(barrier, inc=1, device_id=(p, col), device_id_type=MESH)
    pl.when(has_up)(lambda: greet(p - 1))
    pl.when(has_down)(lambda: greet(p + 1))

    small[0].wait()
    wide = jnp.concatenate([mis[l] for l in range(levels)], axis=1)
    high = wide.astype(jnp.bfloat16).astype(jnp.float32)
    split[0] = high
    split[1] = wide - high

    for copy in small[1:4]:
        copy.wait()
    place = loc[...].astype(jnp.float32)
    radius = (tile * 0.125) * (1.0 + cat[...].astype(jnp.float32))
    radius_sq = radius * radius
    cover = codes[...]
    barred = [
        jnp.where(jnp.any(cover == code, axis=0, keepdims=True), 0.0, 4.0 * half * half)
        for code in range(9)
    ]
    for j in range(4):
        b = lax.broadcasted_iota(jnp.int32, (half, slots), 0).astype(jnp.float32) + (j - 1) * half
        gap = b - place[1:2]
        gap = gap * gap
        ds = (j + 1) // 2
        for dr in range(3):
            bound[dr * 4 + j] = (gap + barred[3 * dr + ds]).astype(jnp.bfloat16)

    diagonal = (
        lax.rem(lax.broadcasted_iota(jnp.int32, (tile, levels * tile), 1), tile)
        == lax.broadcasted_iota(jnp.int32, (tile, levels * tile), 0)
    )

    def remote(src, slot, row, col):
        return pltpu.make_async_remote_copy(
            src_ref=src,
            dst_ref=halo.at[slot],
            send_sem=send_sem.at[slot],
            recv_sem=recv_sem.at[slot],
            device_id=(row, col),
            device_id_type=MESH,
        )

    for stage, yh in enumerate(halves):
        def level_sum(y, _):
            row = yh * half + y
            terms = []
            for s in range(2):
                line = split[s, pl.ds(row, 1), :]
                terms.append(
                    jnp.where(diagonal, jnp.broadcast_to(line, diagonal.shape), 0.0).astype(jnp.bfloat16)
                )
            both = jnp.dot(
                jnp.concatenate(terms, axis=0),
                dev[:, row].reshape(levels * tile, members),
                preferred_element_type=jnp.float32,
            )
            total = both[:tile] + both[tile:]
            cells[0, y] = total[:half]
            cells[1, y] = total[half:]
            return 0

        for c in range(HALF_CHUNKS):
            reads[stage * HALF_CHUNKS + c].wait()
            lax.fori_loop(c * rows_per, (c + 1) * rows_per, level_sum, 0, unroll=True)
        for xh in range(2):
            own[2 * yh + xh] = cells[xh].reshape(half * half, members).T.astype(jnp.bfloat16)
        if stage == 0:
            peers = 2 + 3 * jnp.minimum(p, 1) + 3 * jnp.minimum(nlat - 1 - p, 1)
            pl.semaphore_wait(barrier, peers)
        beyond = p + 2 * yh - 1
        edge = 12 * (1 - yh)
        for xh in range(2):
            j, col = (3, left) if xh == 0 else (0, right)
            mine = 2 * yh + xh
            source = own.at[mine]
            remote(source, 4 * (yh + 1) + j, p, col).start()
            pl.when(present[stage])(remote(source, edge + xh + 1, beyond, q).start)

    def relay(stage, j):
        yh = halves[stage]
        slot = 4 * (yh + 1) + j
        remote(halo.at[slot], slot, p, right).wait_recv()
        copy = remote(halo.at[slot], 12 * (1 - yh) + j, p + 2 * yh - 1, q)
        pl.when(present[stage])(copy.start)

    near = 3 * (1 - jnp.minimum(q, 1))
    copies = {
        slot: remote(own.at[0], slot, p, right)
        for slot in (1, 2, 13, 14, 4, 7, 8, 11, 0, 3, 12, 15)
    }

    row_gap = jnp.broadcast_to(place[0:1], (half, slots)).astype(jnp.bfloat16)
    reach = jnp.broadcast_to(radius_sq, (half, slots)).astype(jnp.bfloat16)
    for i in (1, 2, 0, 3):
        dr = (i + 1) // 2

        def build(y, gap):
            room = reach - gap * gap
            for j in range(4):
                t = jnp.maximum(room - bound[dr * 4 + j], jnp.bfloat16(0))
                taper[i * 4 + j, y] = t * t
            return gap - jnp.bfloat16(1)

        lax.fori_loop(0, half, build, row_gap - jnp.bfloat16((i - 1) * half), unroll=2)

    def product(slot, source):
        return jnp.dot(
            source,
            taper[slot].reshape(half * half, slots),
            preferred_element_type=jnp.float32,
        )

    def add(slot):
        acc[...] += product(slot, halo[slot])

    def receive(slot):
        copies[slot].wait_recv()
        add(slot)

    relay(0, near)
    for yh in range(2):
        for xh in range(2):
            value = product((yh + 1) * 4 + xh + 1, own[2 * yh + xh])
            if yh == 0 and xh == 0:
                acc[...] = value
            else:
                acc[...] += value
    for slot in (1, 2, 13, 14):
        pl.when(has_up if slot < 4 else has_down)(functools.partial(receive, slot))
    relay(1, near)
    relay(0, 3 - near)
    relay(1, 3 - near)
    for yh in range(2):
        for slot in (4 * yh + 4, 4 * yh + 7):
            add(slot)
    for slot in (0, 3, 12, 15):
        pl.when(has_up if slot < 4 else has_down)(functools.partial(receive, slot))

    for copy in small[4:]:
        copy.wait()
    summed = jnp.sum(acc[...] * sens[...].astype(jnp.float32), axis=0, keepdims=True)
    live = lax.broadcasted_iota(jnp.int32, (1, slots), 1) < tally_hbm[0, 0]
    value = scaled[...] * summed / ((members - 1) * radius_sq * radius_sq)
    out_ref[...] = jnp.where(live, value, 0.0)

    for slot, copy in copies.items():
        if slot < 4:
            pl.when(has_down)(copy.wait_send)
        elif slot >= 12:
            pl.when(has_up)(copy.wait_send)
        else:
            copy.wait_send()


def on_device(nlat, nlon, dev, mis, sens, scaled, loc, cat, codes, tally):
    levels, tile, _, members = dev.shape
    slots = sens.shape[3]
    half = tile // 2
    quad = half * half
    bf16, f32, i32 = jnp.bfloat16, jnp.float32, jnp.int32
    out = pl.pallas_call(
        functools.partial(kernel, nlat, nlon),
        out_shape=pltpu.VMEM((1, slots), f32),
        in_specs=[pl.BlockSpec(memory_space=pl.ANY)] * 7 + [pl.BlockSpec(memory_space=pltpu.SMEM)],
        out_specs=pl.BlockSpec(memory_space=pltpu.VMEM),
        scratch_shapes=[
            pltpu.VMEM((levels, tile, tile, members), bf16),
            pltpu.VMEM((levels, tile, tile), f32),
            pltpu.VMEM((members, slots), bf16),
            pltpu.VMEM((1, slots), f32),
            pltpu.VMEM((2, slots), i32),
            pltpu.VMEM((1, slots), i32),
            pltpu.VMEM((4, slots), i32),
            pltpu.VMEM((2, tile, levels * tile), f32),
            pltpu.VMEM((2, half, half, members), f32),
            pltpu.VMEM((4, members, quad), bf16),
            pltpu.VMEM((16, members, quad), bf16),
            pltpu.VMEM((12, half, slots), bf16),
            pltpu.VMEM((16, half, half, slots), bf16),
            pltpu.VMEM((members, slots), f32),
            pltpu.SemaphoreType.DMA((6,)),
            pltpu.SemaphoreType.DMA((2 * HALF_CHUNKS,)),
            pltpu.SemaphoreType.DMA((16,)),
            pltpu.SemaphoreType.DMA((16,)),
        ],
        compiler_params=pltpu.CompilerParams(
            collective_id=0, has_side_effects=True, vmem_limit_bytes=32 * 1024 * 1024
        ),
    )(*[pltpu.with_memory_space_constraint(x, pltpu.HBM) for x in (dev, mis, sens[0, 0], scaled[0], loc[0, 0], cat[0], codes[0, 0])], tally)
    return out[None]


def solution(mesh):
    return jax.shard_map(
        functools.partial(on_device, mesh.shape["lat"], mesh.shape["lon"]),
        mesh=mesh,
        in_specs=(
            P(None, "lat", "lon", None),
            P(None, "lat", "lon"),
            P("lat", "lon", None, None),
            P("lat", "lon", None),
            P("lat", "lon", None, None),
            P("lat", "lon", None),
            P("lat", "lon", None, None),
            P("lat", "lon"),
        ),
        out_specs=P("lat", "lon", None),
        check_vma=False,
    )
```

```python
import functools

import jax
import jax.numpy as jnp
from jax import lax
from jax.experimental import pallas as pl
from jax.experimental.pallas import tpu as pltpu
from jax.sharding import PartitionSpec as P

MESH = pl.DeviceIdType.MESH
PIECES = 2


def kernel(
    nlat, nlon,
    dev_hbm, mis_hbm, sens_hbm, scaled_hbm, loc_hbm, cat_hbm, codes_hbm, tally,
    out_ref,
    dev, mis, sens, scaled, loc, cat, codes,
    lines, own, halo, bound, taper, acc,
    in_sem, dev_sem, send_sem, recv_sem, open_sem,
):
    _, levels, tile, half, members = dev.shape
    slots = sens.shape[1]
    rows_per = half // PIECES
    quad = half * half
    p = lax.axis_index("lat")
    q = lax.axis_index("lon")
    left = lax.rem(q + nlon - 1, nlon)
    right = lax.rem(q + 1, nlon)
    has = (p > 0, p < nlat - 1)
    odd = lax.rem(p, 2)
    cross = p - 1 + 2 * odd
    has_cross = (cross >= 0) & (cross < nlat)
    has_cross_n = jnp.where(has_cross, 1, 0)
    head = q == 0
    tail = q == nlon - 1

    first = jnp.where(head | tail, 1, 0)
    halves = (first, 1 - first)
    small = [
        pltpu.make_async_copy(src, dst, in_sem.at[i])
        for i, (src, dst) in enumerate(
            [(mis_hbm, mis), (loc_hbm, loc), (cat_hbm, cat), (codes_hbm, codes),
             (sens_hbm, sens), (scaled_hbm, scaled)]
        )
    ]
    reads = [
        pltpu.make_async_copy(
            dev_hbm.at[:, pl.ds(r * rows_per, rows_per), pl.ds(pl.multiple_of(xh * half, half), half)],
            dev.at[s, :, pl.ds(r * rows_per, rows_per)],
            dev_sem.at[s * 2 * PIECES + r],
        )
        for s, xh in enumerate(halves)
        for r in range(2 * PIECES)
    ]
    small[0].start()
    for copy in reads:
        copy.start()
    for copy in small[1:]:
        copy.start()

    barrier = pltpu.get_barrier_semaphore()

    def signal(semaphore, row, col):
        pl.semaphore_signal(semaphore, inc=1, device_id=(row, col), device_id_type=MESH)

    pl.when(has[0])(lambda: signal(barrier, p - 1, q))
    pl.when(has[1])(lambda: signal(barrier, p + 1, q))
    signal(barrier, p, left)
    pl.when(jnp.logical_not(tail))(lambda: signal(barrier, p, right))
    pl.when(head & has_cross)(lambda: signal(barrier, cross, left))
    peers = (
        jnp.minimum(p, 1) + jnp.minimum(nlat - 1 - p, 1) + jnp.where(head, 1, 2)
        + jnp.where(tail, has_cross_n, 0)
    )

    small[0].wait()
    for xh in range(2):
        lines[xh] = jnp.concatenate([mis[l, :, xh * half:(xh + 1) * half] for l in range(levels)], axis=1)

    diagonal = (
        lax.rem(lax.broadcasted_iota(jnp.int32, (half, levels * half), 1), half)
        == lax.broadcasted_iota(jnp.int32, (half, levels * half), 0)
    )

    def remote(src, slot, c, kind, which, row, col):
        return pltpu.make_async_remote_copy(
            src_ref=src,
            dst_ref=halo.at[slot, c],
            send_sem=send_sem.at[(kind * 4 + which) * PIECES + c],
            recv_sem=recv_sem.at[slot * PIECES + c],
            device_id=(row, col),
            device_id_type=MESH,
        )

    def beside(yh, c, xh):
        mine = 2 * yh + xh
        return remote(own.at[mine, c], 4 * (yh + 1) + 3 * (1 - xh), c, 0, mine, p, jnp.where(xh == 0, left, right))

    def across(yh, c, xh):
        mine = 2 * yh + xh
        return remote(own.at[mine, c], 12 * (1 - yh) + 1 + xh, c, 1, mine, p + 2 * yh - 1, q)

    def corner(yh, c, xh):
        mine = 2 * yh + xh
        return remote(own.at[mine, c], 12 * (1 - yh) + 3 * (1 - xh), c, 2, mine, p + 2 * yh - 1, jnp.where(xh == 0, left, right))

    def far_row(yh):
        return has_cross & (odd == yh)

    for s, xh in enumerate(halves):
        for r in range(2 * PIECES):
            yh, c = divmod(r, PIECES)
            reads[s * 2 * PIECES + r].wait()
            sums = []
            for y in range(r * rows_per, (r + 1) * rows_per):
                line = lines[xh, pl.ds(y, 1), :]
                spread = jnp.where(diagonal, jnp.broadcast_to(line, diagonal.shape), 0.0)
                high = spread.astype(jnp.bfloat16)
                low = (spread - high.astype(jnp.float32)).astype(jnp.bfloat16)
                both = jnp.dot(
                    jnp.concatenate([high, low], axis=0),
                    dev[s, :, y].reshape(levels * half, members),
                    preferred_element_type=jnp.float32,
                )
                sums.append(both[:half] + both[half:])
            own[2 * yh + xh, c] = jnp.concatenate(sums, axis=0).T.astype(jnp.bfloat16)
            if s == 0 and r == 0:
                pl.semaphore_wait(barrier, peers)

                @pl.when(tail)
                def _():
                    signal(open_sem, p, right)
                    pl.when(has_cross)(lambda: signal(open_sem, cross, right))

            if s == 0:
                beside(yh, c, xh).start()
                pl.when(tail & far_row(yh))(corner(yh, c, xh).start)
            else:
                pl.when(jnp.logical_not(head))(beside(yh, c, xh).start)
            pl.when(has[yh])(across(yh, c, xh).start)

    for copy in small[1:4]:
        copy.wait()
    place = loc[...].astype(jnp.float32)
    radius = (tile * 0.125) * (1.0 + cat[...].astype(jnp.float32))
    radius_sq = radius * radius
    cover = codes[...]
    barred = [
        jnp.where(jnp.any(cover == code, axis=0, keepdims=True), 0.0, 4.0 * half * half)
        for code in range(9)
    ]
    for j in range(4):
        b = lax.broadcasted_iota(jnp.int32, (half, slots), 0).astype(jnp.float32) + (j - 1) * half
        gap = b - place[1:2]
        gap = gap * gap
        ds = (j + 1) // 2
        for dr in range(3):
            bound[dr * 4 + j] = (gap + barred[3 * dr + ds]).astype(jnp.bfloat16)

    row_gap = jnp.broadcast_to(place[0:1], (half, slots)).astype(jnp.bfloat16)
    reach = jnp.broadcast_to(radius_sq, (half, slots)).astype(jnp.bfloat16)
    for i in (1, 2, 0, 3):
        dr = (i + 1) // 2

        def build(y, gap):
            room = reach - gap * gap
            for j in range(4):
                t = jnp.maximum(room - bound[dr * 4 + j], jnp.bfloat16(0))
                taper[i * 4 + j, y] = t * t
            return gap - jnp.bfloat16(1)

        lax.fori_loop(0, half, build, row_gap - jnp.bfloat16((i - 1) * half), unroll=2)

    def product(slot, source):
        return jnp.dot(
            jnp.concatenate([source[c] for c in range(PIECES)], axis=1),
            taper[slot].reshape(quad, slots),
            preferred_element_type=jnp.float32,
        )

    def add(slot):
        acc[...] += product(slot, halo[slot])

    def arrive(slot, c):
        remote(own.at[0, c], slot, c, 0, 0, p, right).wait_recv()

    def receive(slot):
        for c in range(PIECES):
            arrive(slot, c)
        add(slot)

    near = jnp.where(head, 3, 0)
    far = 3 - near

    def relayed(yh, j):
        wrapped = (head & (j == 0)) | (tail & (j == 3))
        return has[yh] & jnp.logical_not(wrapped & (odd == yh))

    def relay_copy(yh, j, c):
        slot = 4 * (yh + 1) + j
        return remote(halo.at[slot, c], 12 * (1 - yh) + j, c, 3, 2 * yh + jnp.where(j == 0, 0, 1), p + 2 * yh - 1, q)

    def relay(j):
        for yh in range(2):
            for c in range(PIECES):
                arrive(4 * (yh + 1) + j, c)
                pl.when(relayed(yh, j))(relay_copy(yh, j, c).start)

    for yh in range(2):
        for xh in range(2):
            value = product((yh + 1) * 4 + xh + 1, own[2 * yh + xh])
            if yh == 0 and xh == 0:
                acc[...] = value
            else:
                acc[...] += value
    relay(near)

    @pl.when(head)
    def _():
        pl.semaphore_wait(open_sem, 1 + has_cross_n)
        for yh in range(2):
            for c in range(PIECES):
                beside(yh, c, 0).start()
                pl.when(far_row(yh))(corner(yh, c, 0).start)

    for slot in (1, 2, 13, 14):
        pl.when(has[slot // 12])(functools.partial(receive, slot))
    for yh in range(2):
        add(4 * (yh + 1) + near)
    relay(far)
    for yh in range(2):
        add(4 * (yh + 1) + far)
    for j in (near, far):
        for yh in range(2):
            pl.when(has[yh])(functools.partial(receive, 12 * yh + j))

    for copy in small[4:]:
        copy.wait()
    summed = jnp.sum(acc[...] * sens[...].astype(jnp.float32), axis=0, keepdims=True)
    live = lax.broadcasted_iota(jnp.int32, (1, slots), 1) < tally[0, 0]
    value = scaled[...] * summed / ((members - 1) * radius_sq * radius_sq)
    out_ref[...] = jnp.where(live, value, 0.0)

    for yh in range(2):
        for c in range(PIECES):
            for xh in range(2):
                beside(yh, c, xh).wait_send()
                pl.when(has[yh])(across(yh, c, xh).wait_send)
                edge = head if xh == 0 else tail
                pl.when(edge & far_row(yh))(corner(yh, c, xh).wait_send)
                pl.when(relayed(yh, 3 * xh))(relay_copy(yh, 3 * xh, c).wait_send)


def on_device(nlat, nlon, dev, mis, sens, scaled, loc, cat, codes, tally):
    levels, tile, _, members = dev.shape
    slots = sens.shape[3]
    half = tile // 2
    quad = half * half
    bf16, f32, i32 = jnp.bfloat16, jnp.float32, jnp.int32
    operands = [
        pltpu.with_memory_space_constraint(x, pltpu.HBM)
        for x in (dev, mis, sens[0, 0], scaled[0], loc[0, 0], cat[0], codes[0, 0])
    ]
    out = pl.pallas_call(
        functools.partial(kernel, nlat, nlon),
        out_shape=pltpu.VMEM((1, slots), f32),
        in_specs=[pl.BlockSpec(memory_space=pl.ANY)] * 7 + [pl.BlockSpec(memory_space=pltpu.SMEM)],
        out_specs=pl.BlockSpec(memory_space=pltpu.VMEM),
        scratch_shapes=[
            pltpu.VMEM((2, levels, tile, half, members), bf16),
            pltpu.VMEM((levels, tile, tile), f32),
            pltpu.VMEM((members, slots), bf16),
            pltpu.VMEM((1, slots), f32),
            pltpu.VMEM((2, slots), i32),
            pltpu.VMEM((1, slots), i32),
            pltpu.VMEM((4, slots), i32),
            pltpu.VMEM((2, tile, levels * half), f32),
            pltpu.VMEM((4, PIECES, members, quad // PIECES), bf16),
            pltpu.VMEM((16, PIECES, members, quad // PIECES), bf16),
            pltpu.VMEM((12, half, slots), bf16),
            pltpu.VMEM((16, half, half, slots), bf16),
            pltpu.VMEM((members, slots), f32),
            pltpu.SemaphoreType.DMA((6,)),
            pltpu.SemaphoreType.DMA((4 * PIECES,)),
            pltpu.SemaphoreType.DMA((16 * PIECES,)),
            pltpu.SemaphoreType.DMA((16 * PIECES,)),
            pltpu.SemaphoreType.REGULAR,
        ],
        compiler_params=pltpu.CompilerParams(
            collective_id=0, has_side_effects=True, vmem_limit_bytes=32 * 1024 * 1024
        ),
    )(*operands, tally)
    return out[None]


def solution(mesh):
    return jax.shard_map(
        functools.partial(on_device, mesh.shape["lat"], mesh.shape["lon"]),
        mesh=mesh,
        in_specs=(
            P(None, "lat", "lon", None),
            P(None, "lat", "lon"),
            P("lat", "lon", None, None),
            P("lat", "lon", None),
            P("lat", "lon", None, None),
            P("lat", "lon", None),
            P("lat", "lon", None, None),
            P("lat", "lon"),
        ),
        out_specs=P("lat", "lon", None),
        check_vma=False,
    )
```

```python
import functools

import jax
import jax.numpy as jnp
from jax import lax
from jax.experimental import pallas as pl
from jax.experimental.pallas import tpu as pltpu
from jax.sharding import PartitionSpec as P

MESH = pl.DeviceIdType.MESH
PIECES = 2


def kernel(
    nlat, nlon,
    dev_hbm, mis_hbm, sens_hbm, scaled_hbm, loc_hbm, cat_hbm, codes_hbm, tally,
    out_ref,
    dev, mis, sens, scaled, loc, cat, codes,
    lines, own, halo, bound, taper, acc,
    in_sem, mis_sem, dev_sem, send_sem, recv_sem, open_sem,
):
    _, levels, tile, half, members = dev.shape
    steps = 2 * PIECES
    slots = sens.shape[1]
    rows_per = half // PIECES
    quad = half * half
    p = lax.axis_index("lat")
    q = lax.axis_index("lon")
    left = lax.rem(q + nlon - 1, nlon)
    right = lax.rem(q + 1, nlon)
    has_up, has_down = p > 0, p < nlat - 1
    odd = lax.rem(p, 2)
    cross = p - 1 + 2 * odd
    has_cross = (cross >= 0) & (cross < nlat)
    has_cross_n = jnp.where(has_cross, 1, 0)
    head = q == 0
    tail = q == nlon - 1

    first = jnp.where(head | tail, 1, 0)
    halves = (first, 1 - first)
    lead = jnp.where(has_cross, odd, 1 - odd)
    bands = (lead, 1 - lead)

    def has(yh):
        return (yh == 0) & has_up | (yh == 1) & has_down

    parts = [(s, r, xh, bands[r // PIECES], r % PIECES) for s, xh in enumerate(halves) for r in range(steps)]
    small = [
        pltpu.make_async_copy(src, dst, in_sem.at[i])
        for i, (src, dst) in enumerate(
            [(loc_hbm, loc), (cat_hbm, cat), (codes_hbm, codes),
             (sens_hbm, sens), (scaled_hbm, scaled)]
        )
    ]
    reads = [
        pltpu.make_async_copy(
            dev_hbm.at[:, pl.ds(yh * half + c * rows_per, rows_per), pl.ds(pl.multiple_of(xh * half, half), half)],
            dev.at[s, :, pl.ds(r * rows_per, rows_per)],
            dev_sem.at[s * steps + r],
        )
        for s, r, xh, yh, c in parts
    ]
    weights = pltpu.make_async_copy(mis_hbm, mis, mis_sem)
    weights.start()
    for copy in reads + small:
        copy.start()

    barrier = pltpu.get_barrier_semaphore()

    def signal(semaphore, row, col):
        pl.semaphore_signal(semaphore, inc=1, device_id=(row, col), device_id_type=MESH)

    pl.when(has_up)(lambda: signal(barrier, p - 1, q))
    pl.when(has_down)(lambda: signal(barrier, p + 1, q))
    signal(barrier, p, left)
    pl.when(jnp.logical_not(tail))(lambda: signal(barrier, p, right))
    pl.when((head | (odd == 1)) & has_cross)(lambda: signal(barrier, cross, left))
    pl.when(jnp.logical_not(tail) & (odd == 1) & has_cross)(lambda: signal(barrier, cross, right))
    peers = (
        jnp.minimum(p, 1) + jnp.minimum(nlat - 1 - p, 1) + jnp.where(head, 1, 2)
        + jnp.where(tail, has_cross_n, 0)
        + jnp.where(odd == 0, has_cross_n, 0) * (jnp.minimum(q, 1) + jnp.minimum(nlon - 1 - q, 1))
    )

    def enter():
        pl.semaphore_wait(barrier, peers)

        @pl.when(tail)
        def _():
            signal(open_sem, p, right)
            pl.when(has_cross)(lambda: signal(open_sem, cross, right))

    soon = tail & (odd == 0)
    pl.when(soon)(enter)

    weights.wait()
    for xh in range(2):
        lines[xh] = jnp.concatenate([mis[l, :, xh * half:(xh + 1) * half] for l in range(levels)], axis=1)

    diagonal = (
        lax.rem(lax.broadcasted_iota(jnp.int32, (half, levels * half), 1), half)
        == lax.broadcasted_iota(jnp.int32, (half, levels * half), 0)
    )

    def remote(src, slot, c, kind, which, row, col):
        return pltpu.make_async_remote_copy(
            src_ref=src,
            dst_ref=halo.at[slot, c],
            send_sem=send_sem.at[(kind * 4 + which) * PIECES + c],
            recv_sem=recv_sem.at[slot * PIECES + c],
            device_id=(row, col),
            device_id_type=MESH,
        )

    def beside(yh, c, xh):
        mine = 2 * yh + xh
        return remote(own.at[mine, c], 4 * (yh + 1) + 3 * (1 - xh), c, 0, mine, p, jnp.where(xh == 0, left, right))

    def across(yh, c, xh):
        mine = 2 * yh + xh
        return remote(own.at[mine, c], 12 * (1 - yh) + 1 + xh, c, 1, mine, p + 2 * yh - 1, q)

    def corner(yh, c, xh):
        mine = 2 * yh + xh
        return remote(own.at[mine, c], 12 * (1 - yh) + 3 * (1 - xh), c, 2, mine, p + 2 * yh - 1, jnp.where(xh == 0, left, right))

    def far_row(yh):
        return has_cross & (odd == yh)

    def direct(xh):
        return (odd == 0) | (head & (xh == 0))

    def project(s, r, xh, yh, c):
        rows = lines[xh, pl.ds(pl.multiple_of(yh * half + c * rows_per, rows_per), rows_per), :]
        reads[s * steps + r].wait()
        sums = []
        for y in range(rows_per):
            spread = jnp.where(diagonal, jnp.broadcast_to(rows[y:y + 1], diagonal.shape), 0.0)
            high = spread.astype(jnp.bfloat16)
            low = (spread - high.astype(jnp.float32)).astype(jnp.bfloat16)
            both = jnp.dot(
                jnp.concatenate([high, low], axis=0),
                dev[s, :, r * rows_per + y].reshape(levels * half, members),
                preferred_element_type=jnp.float32,
            )
            sums.append(both[:half] + both[half:])
        return jnp.concatenate(sums, axis=0)

    def share(s, r, xh, yh, c, value):
        own[2 * yh + xh, c] = value.T.astype(jnp.bfloat16)
        if s == 0 and r == 0:
            pl.when(jnp.logical_not(soon))(enter)

        wrapped = head & (xh == 0)
        pl.when(direct(xh) & far_row(yh) & jnp.logical_not(wrapped))(corner(yh, c, xh).start)
        if s == 0:
            beside(yh, c, xh).start()
        else:
            pl.when(jnp.logical_not(wrapped))(beside(yh, c, xh).start)
        pl.when(has(yh))(across(yh, c, xh).start)

    value = project(*parts[0])
    for part, following in zip(parts, parts[1:] + [None]):
        if following is not None:
            later = project(*following)
        share(*part, value)
        value = later

    for copy in small[:3]:
        copy.wait()
    place = loc[...].astype(jnp.float32)
    radius = (tile * 0.125) * (1.0 + cat[...].astype(jnp.float32))
    radius_sq = radius * radius
    cover = codes[...]
    barred = [
        jnp.where(jnp.any(cover == code, axis=0, keepdims=True), 0.0, 4.0 * half * half)
        for code in range(9)
    ]
    for j in range(4):
        b = lax.broadcasted_iota(jnp.int32, (half, slots), 0).astype(jnp.float32) + (j - 1) * half
        gap = b - place[1:2]
        gap = gap * gap
        ds = (j + 1) // 2
        for dr in range(3):
            bound[dr * 4 + j] = (gap + barred[3 * dr + ds]).astype(jnp.bfloat16)

    row_gap = jnp.broadcast_to(place[0:1], (half, slots)).astype(jnp.bfloat16)
    reach = jnp.broadcast_to(radius_sq, (half, slots)).astype(jnp.bfloat16)
    for i in (1, 2, 0, 3):
        dr = (i + 1) // 2

        def build(y, gap):
            room = reach - gap * gap
            for j in range(4):
                t = jnp.maximum(room - bound[dr * 4 + j], jnp.bfloat16(0))
                taper[i * 4 + j, y] = t * t
            return gap - jnp.bfloat16(1)

        lax.fori_loop(0, half, build, row_gap - jnp.bfloat16((i - 1) * half), unroll=2)

    def product(slot, source):
        return jnp.dot(
            jnp.concatenate([source[c] for c in range(PIECES)], axis=1),
            taper[slot].reshape(quad, slots),
            preferred_element_type=jnp.float32,
        )

    def add(slot):
        acc[...] += product(slot, halo[slot])

    def arrive(slot, c):
        remote(own.at[0, c], slot, c, 0, 0, p, right).wait_recv()

    def receive(slot):
        for c in range(PIECES):
            arrive(slot, c)
        add(slot)

    near = jnp.where(head, 3, 0)
    far = 3 - near

    def relayed(yh, j):
        sent = (odd == 0) | (tail & (j == 3))
        return has(yh) & jnp.logical_not(sent & (odd == yh))

    def relay_copy(yh, j, c):
        slot = 4 * (yh + 1) + j
        return remote(halo.at[slot, c], 12 * (1 - yh) + j, c, 3, 2 * yh + jnp.where(j == 0, 0, 1), p + 2 * yh - 1, q)

    def relay(j, yh):
        for c in range(PIECES):
            arrive(4 * (yh + 1) + j, c)
            pl.when(relayed(yh, j))(relay_copy(yh, j, c).start)

    def add_corner(j, yh):
        pl.when(has(yh))(functools.partial(receive, 12 * yh + j))

    inner = jnp.logical_not(head | tail)
    lag = 1 - lead
    @pl.when(head)
    def _():
        pl.semaphore_wait(open_sem, 1 + has_cross_n)
        for yh in bands:
            for c in range(PIECES):
                pl.when(far_row(yh))(corner(yh, c, 0).start)
                beside(yh, c, 0).start()

    ahead = (odd == 1) & inner
    pl.when(odd == 1)(lambda: relay(near, lead))
    pl.when(ahead)(lambda: relay(far, lead))
    for yh in range(2):
        for xh in range(2):
            value = product((yh + 1) * 4 + xh + 1, own[2 * yh + xh])
            if yh == 0 and xh == 0:
                acc[...] = value
            else:
                acc[...] += value
    pl.when(odd == 0)(lambda: relay(near, lead))
    relay(near, lag)
    for slot in (1, 2, 13, 14):
        pl.when(has(slot // 12))(functools.partial(receive, slot))
    for yh in range(2):
        add(4 * (yh + 1) + near)
    pl.when(jnp.logical_not(ahead))(lambda: relay(far, lead))
    add(4 * (lead + 1) + far)
    relay(far, lag)
    add(4 * (lag + 1) + far)
    last = jnp.where(odd == 1, lag, lead)
    for j in (near, far):
        for yh in (1 - last, last):
            add_corner(j, yh)

    for copy in small[3:]:
        copy.wait()
    summed = jnp.sum(acc[...] * sens[...].astype(jnp.float32), axis=0, keepdims=True)
    live = lax.broadcasted_iota(jnp.int32, (1, slots), 1) < tally[0, 0]
    value = scaled[...] * summed / ((members - 1) * radius_sq * radius_sq)
    out_ref[...] = jnp.where(live, value, 0.0)

    for yh in range(2):
        for c in range(PIECES):
            for xh in range(2):
                beside(yh, c, xh).wait_send()
                pl.when(has(yh))(across(yh, c, xh).wait_send)
                pl.when(direct(xh) & far_row(yh))(corner(yh, c, xh).wait_send)
                pl.when(relayed(yh, 3 * xh))(relay_copy(yh, 3 * xh, c).wait_send)


def on_device(nlat, nlon, dev, mis, sens, scaled, loc, cat, codes, tally):
    levels, tile, _, members = dev.shape
    slots = sens.shape[3]
    half = tile // 2
    quad = half * half
    bf16, f32, i32 = jnp.bfloat16, jnp.float32, jnp.int32
    operands = [
        pltpu.with_memory_space_constraint(x, pltpu.HBM)
        for x in (dev, mis, sens[0, 0], scaled[0], loc[0, 0], cat[0], codes[0, 0])
    ]
    out = pl.pallas_call(
        functools.partial(kernel, nlat, nlon),
        out_shape=pltpu.VMEM((1, slots), f32),
        in_specs=[pl.BlockSpec(memory_space=pl.ANY)] * 7 + [pl.BlockSpec(memory_space=pltpu.SMEM)],
        out_specs=pl.BlockSpec(memory_space=pltpu.VMEM),
        scratch_shapes=[
            pltpu.VMEM((2, levels, tile, half, members), bf16),
            pltpu.VMEM((levels, tile, tile), f32),
            pltpu.VMEM((members, slots), bf16),
            pltpu.VMEM((1, slots), f32),
            pltpu.VMEM((2, slots), i32),
            pltpu.VMEM((1, slots), i32),
            pltpu.VMEM((4, slots), i32),
            pltpu.VMEM((2, tile, levels * half), f32),
            pltpu.VMEM((4, PIECES, members, quad // PIECES), bf16),
            pltpu.VMEM((16, PIECES, members, quad // PIECES), bf16),
            pltpu.VMEM((12, half, slots), bf16),
            pltpu.VMEM((16, half, half, slots), bf16),
            pltpu.VMEM((members, slots), f32),
            pltpu.SemaphoreType.DMA((5,)),
            pltpu.SemaphoreType.DMA,
            pltpu.SemaphoreType.DMA((4 * PIECES,)),
            pltpu.SemaphoreType.DMA((16 * PIECES,)),
            pltpu.SemaphoreType.DMA((16 * PIECES,)),
            pltpu.SemaphoreType.REGULAR,
        ],
        compiler_params=pltpu.CompilerParams(
            collective_id=0, has_side_effects=True, vmem_limit_bytes=32 * 1024 * 1024
        ),
    )(*operands, tally)
    return out[None]


def solution(mesh):
    return jax.shard_map(
        functools.partial(on_device, mesh.shape["lat"], mesh.shape["lon"]),
        mesh=mesh,
        in_specs=(
            P(None, "lat", "lon", None),
            P(None, "lat", "lon"),
            P("lat", "lon", None, None),
            P("lat", "lon", None),
            P("lat", "lon", None, None),
            P("lat", "lon", None),
            P("lat", "lon", None, None),
            P("lat", "lon"),
        ),
        out_specs=P("lat", "lon", None),
        check_vma=False,
    )
```

```python
import functools

import jax
import jax.numpy as jnp
from jax import lax
from jax.experimental import pallas as pl
from jax.experimental.pallas import tpu as pltpu
from jax.sharding import PartitionSpec as P

MESH = pl.DeviceIdType.MESH
PIECES = 2


def kernel(
    nlat, nlon,
    dev_hbm, mis_hbm, sens_hbm, scaled_hbm, loc_hbm, cat_hbm, codes_hbm, tally,
    out_ref,
    dev, mis, sens, scaled, loc, cat, codes,
    lines, own, halo, bound, taper, acc,
    read_sem, send_sem, recv_sem, open_sem,
):
    _, levels, tile, half, members = dev.shape
    slots = sens.shape[1]
    steps = 2 * PIECES
    rows_per = half // PIECES
    quad = half * half
    p = lax.axis_index("lat")
    q = lax.axis_index("lon")
    left = lax.rem(q + nlon - 1, nlon)
    right = lax.rem(q + 1, nlon)
    has_up, has_down = p > 0, p < nlat - 1
    odd = lax.rem(p, 2)
    cross = p - 1 + 2 * odd
    has_cross = (cross >= 0) & (cross < nlat)
    has_cross_n = jnp.where(has_cross, 1, 0)
    head = q == 0
    tail = q == nlon - 1

    first = jnp.where(head | tail, 1, 0)
    halves = (first, 1 - first)
    hold = has_cross & (odd == 0)
    lead = jnp.where(has_down, 1, 0)
    lag = 1 - lead
    opening = jnp.where(hold, 0, lead)
    bands = (opening, 1 - opening)

    def has(yh):
        return (yh == 0) & has_up | (yh == 1) & has_down

    parts = [(s, r, xh, bands[r // PIECES], r % PIECES) for s, xh in enumerate(halves) for r in range(steps)]

    def columns(xh):
        return pl.ds(pl.multiple_of(xh * half, half), half)

    def local(src, dst, i):
        return pltpu.make_async_copy(src, dst, read_sem.at[i])

    weights = local(mis_hbm, mis, 0)
    reads = [
        local(
            dev_hbm.at[:, pl.ds(yh * half + c * rows_per, rows_per), columns(xh)],
            dev.at[0, :, pl.ds(r * rows_per, rows_per)],
            1 + r,
        )
        for s, r, xh, yh, c in parts[:steps]
    ]
    rest = local(dev_hbm.at[:, :, columns(halves[1])], dev.at[1], 1 + steps)
    small = [
        local(src, dst, i)
        for i, (src, dst) in enumerate(
            [(scaled_hbm, scaled), (loc_hbm, loc), (cat_hbm, cat), (codes_hbm, codes), (sens_hbm, sens)]
        )
    ]
    for copy in [weights] + reads + [rest]:
        copy.start()

    barrier = pltpu.get_barrier_semaphore()

    def signal(semaphore, row, col):
        pl.semaphore_signal(semaphore, inc=1, device_id=(row, col), device_id_type=MESH)

    pl.when(has_up)(lambda: signal(barrier, p - 1, q))
    pl.when(has_down)(lambda: signal(barrier, p + 1, q))
    signal(barrier, p, left)
    pl.when(jnp.logical_not(tail))(lambda: signal(barrier, p, right))
    pl.when((head | (odd == 1)) & has_cross)(lambda: signal(barrier, cross, left))
    pl.when(jnp.logical_not(tail) & (odd == 1) & has_cross)(lambda: signal(barrier, cross, right))
    peers = (
        jnp.minimum(p, 1) + jnp.minimum(nlat - 1 - p, 1) + jnp.where(head, 1, 2)
        + jnp.where(tail, has_cross_n, 0)
        + jnp.where(odd == 0, has_cross_n, 0) * (jnp.minimum(q, 1) + jnp.minimum(nlon - 1 - q, 1))
    )

    def enter():
        pl.semaphore_wait(barrier, peers)

        @pl.when(tail)
        def _():
            signal(open_sem, p, right)
            pl.when((odd == 1) & has_cross)(lambda: signal(open_sem, cross, right))

    soon = tail & (odd == 0)
    pl.when(soon)(enter)

    weights.wait()
    small[0].start()
    for xh in range(2):
        lines[xh] = jnp.concatenate([mis[l, :, xh * half:(xh + 1) * half] for l in range(levels)], axis=1)

    diagonal = (
        lax.rem(lax.broadcasted_iota(jnp.int32, (half, levels * half), 1), half)
        == lax.broadcasted_iota(jnp.int32, (half, levels * half), 0)
    )

    def remote(src, dst, send, recv, row, col):
        return pltpu.make_async_remote_copy(
            src_ref=src,
            dst_ref=dst,
            send_sem=send_sem.at[send],
            recv_sem=recv_sem.at[recv],
            device_id=(row, col),
            device_id_type=MESH,
        )

    def beside(yh, c, xh):
        dst = halo.at[4 * (yh + 1) + 3 * (1 - xh), c]
        return remote(own.at[2 * yh + xh, c], dst, 0, 2 + 2 * yh + 1 - xh, p, jnp.where(xh == 0, left, right))

    def across(yh, c, xh):
        return remote(own.at[2 * yh + xh, c], halo.at[12 * (1 - yh) + 1 + xh, c], 1 + yh, 1 - yh, p + 2 * yh - 1, q)

    def corner(c, xh):
        return remote(own.at[xh, c], halo.at[12 + 3 * (1 - xh), c], 3, 9 - xh, p - 1, jnp.where(xh == 0, left, right))

    def relay_copy(yh, w):
        return remote(halo.at[4 * (yh + 1) + 3 * w], halo.at[12 * (1 - yh) + 3 * w], 4 + yh, 8 - 2 * yh + w, p + 2 * yh - 1, q)

    def project(s, r, xh, yh, c):
        rows = lines[xh, pl.ds(pl.multiple_of(yh * half + c * rows_per, rows_per), rows_per), :]
        if s == 0:
            reads[r].wait()
            small[1 + r].start()
            top = r * rows_per
        else:
            if r == 0:
                rest.wait()
            top = yh * half + c * rows_per
        sums = []
        for y in range(rows_per):
            spread = jnp.where(diagonal, jnp.broadcast_to(rows[y:y + 1], diagonal.shape), 0.0)
            high = spread.astype(jnp.bfloat16)
            low = (spread - high.astype(jnp.float32)).astype(jnp.bfloat16)
            both = jnp.dot(
                jnp.concatenate([high, low], axis=0),
                dev[s, :, top + y].reshape(levels * half, members),
                preferred_element_type=jnp.float32,
            )
            sums.append(both[:half] + both[half:])
        return jnp.concatenate(sums, axis=0)

    def share(s, r, xh, yh, c, value):
        own[2 * yh + xh, c] = value.T.astype(jnp.bfloat16)
        if s == 0 and r == 0:
            pl.when(jnp.logical_not(soon))(enter)

        wrapped = head & (xh == 0)
        if r < PIECES:
            pl.when(hold & jnp.logical_not(wrapped))(corner(c, xh).start)
            pl.when(jnp.logical_not(hold | wrapped))(beside(yh, c, xh).start)
        else:
            pl.when(jnp.logical_not(wrapped))(beside(yh, c, xh).start)
        pl.when(has(yh))(across(yh, c, xh).start)
        if r == steps - 1:
            for k in range(PIECES):
                pl.when(hold & jnp.logical_not(wrapped))(beside(bands[0], k, xh).start)

    value = project(*parts[0])
    for part, following in zip(parts, parts[1:] + [None]):
        if following is not None:
            later = project(*following)
        share(*part, value)
        value = later

    for copy in small[1:4]:
        copy.wait()
    place = loc[...].astype(jnp.float32)
    radius = (tile * 0.125) * (1.0 + cat[...].astype(jnp.float32))
    radius_sq = radius * radius
    cover = codes[...]
    barred = [
        jnp.where(jnp.any(cover == code, axis=0, keepdims=True), 0.0, 4.0 * half * half)
        for code in range(9)
    ]
    for j in range(4):
        b = lax.broadcasted_iota(jnp.int32, (half, slots), 0).astype(jnp.float32) + (j - 1) * half
        gap = b - place[1:2]
        gap = gap * gap
        ds = (j + 1) // 2
        for dr in range(3):
            bound[dr * 4 + j] = (gap + barred[3 * dr + ds]).astype(jnp.bfloat16)

    row_gap = jnp.broadcast_to(place[0:1], (half, slots)).astype(jnp.bfloat16)
    reach = jnp.broadcast_to(radius_sq, (half, slots)).astype(jnp.bfloat16)
    for i in (1, 2, 0, 3):
        dr = (i + 1) // 2

        def build(y, gap):
            room = reach - gap * gap
            for j in range(4):
                t = jnp.maximum(room - bound[dr * 4 + j], jnp.bfloat16(0))
                taper[i * 4 + j, y] = t * t
            return gap - jnp.bfloat16(1)

        lax.fori_loop(0, half, build, row_gap - jnp.bfloat16((i - 1) * half), unroll=2)

    def product(slot, source):
        return jnp.dot(
            jnp.concatenate([source[c] for c in range(PIECES)], axis=1),
            taper[slot].reshape(quad, slots),
            preferred_element_type=jnp.float32,
        )

    def add(slot):
        acc[...] += product(slot, halo[slot])

    def add_band(yh):
        slot = 12 * yh + 1
        remote(own.at[pl.ds(0, 2)], halo.at[pl.ds(slot, 2)], 0, yh, p, right).wait_recv()
        for xh in range(2):
            add(slot + xh)

    def add_side(yh, w):
        add(4 * (yh + 1) + 3 * w)

    def add_corner(yh, w):
        slot = 12 * yh + 3 * w
        remote(own.at[0], halo.at[slot], 0, 6 + 2 * yh + w, p, right).wait_recv()
        add(slot)

    def relayed(yh):
        return (yh == 0) & has_up & (odd == 1) | (yh == 1) & has_down

    def relay(yh, w):
        remote(own.at[0], halo.at[4 * (yh + 1) + 3 * w], 0, 2 + 2 * yh + w, p, right).wait_recv()
        pl.when(relayed(yh))(relay_copy(yh, w).start)

    near = jnp.where(head, 1, 0)
    far = 1 - near

    @pl.when(head)
    def _():
        pl.semaphore_wait(open_sem, 1 + jnp.where(hold, 1, 0))
        for c in range(PIECES):
            pl.when(hold)(corner(c, 0).start)
        for yh in (lead, lag):
            for c in range(PIECES):
                beside(yh, c, 0).start()

    ahead = (odd == 1) & jnp.logical_not(head | tail)
    pl.when(odd == 1)(lambda: relay(lead, near))
    pl.when(ahead)(lambda: relay(lead, far))
    for yh in range(2):
        for xh in range(2):
            value = product((yh + 1) * 4 + xh + 1, own[2 * yh + xh])
            if yh == 0 and xh == 0:
                acc[...] = value
            else:
                acc[...] += value
    pl.when(has(1 - odd))(lambda: add_band(1 - odd))
    pl.when((odd == 0) & has_up)(lambda: add_band(0))
    pl.when(odd == 0)(lambda: relay(lead, near))
    relay(lag, near)
    for yh in range(2):
        add_side(yh, near)
    pl.when(jnp.logical_not(ahead))(lambda: relay(lead, far))
    pl.when((odd == 1) & has_down)(lambda: add_band(1))
    add_side(lead, far)
    for yh in range(2):
        pl.when(has(yh))(functools.partial(add_corner, yh, near))
    mate = (odd == 0) & has_down
    pl.when(mate)(lambda: add_corner(1, far))
    relay(lag, far)
    add_side(lag, far)
    pl.when(has_up)(lambda: add_corner(0, far))
    pl.when(has_down & jnp.logical_not(mate))(lambda: add_corner(1, far))

    small[0].wait()
    small[4].wait()
    summed = jnp.sum(acc[...] * sens[...].astype(jnp.float32), axis=0, keepdims=True)
    live = lax.broadcasted_iota(jnp.int32, (1, slots), 1) < tally[0, 0]
    value = scaled[...] * summed / ((members - 1) * radius_sq * radius_sq)
    out_ref[...] = jnp.where(live, value, 0.0)

    remote(own, halo.at[pl.ds(0, 4)], 0, 0, p, right).wait_send()

    def sent(i):
        remote(own.at[pl.ds(0, 2)], halo.at[pl.ds(0, 2)], i, 0, p, right).wait_send()

    for yh in range(2):
        pl.when(has(yh))(functools.partial(sent, 1 + yh))
        pl.when(relayed(yh))(functools.partial(sent, 4 + yh))
    pl.when(hold)(functools.partial(sent, 3))


def on_device(nlat, nlon, dev, mis, sens, scaled, loc, cat, codes, tally):
    levels, tile, _, members = dev.shape
    slots = sens.shape[3]
    half = tile // 2
    quad = half * half
    bf16, f32, i32 = jnp.bfloat16, jnp.float32, jnp.int32
    operands = [
        pltpu.with_memory_space_constraint(x, pltpu.HBM)
        for x in (dev, mis, sens[0, 0], scaled[0], loc[0, 0], cat[0], codes[0, 0])
    ]
    out = pl.pallas_call(
        functools.partial(kernel, nlat, nlon),
        out_shape=pltpu.VMEM((1, slots), f32),
        in_specs=[pl.BlockSpec(memory_space=pl.ANY)] * 7 + [pl.BlockSpec(memory_space=pltpu.SMEM)],
        out_specs=pl.BlockSpec(memory_space=pltpu.VMEM),
        scratch_shapes=[
            pltpu.VMEM((2, levels, tile, half, members), bf16),
            pltpu.VMEM((levels, tile, tile), f32),
            pltpu.VMEM((members, slots), bf16),
            pltpu.VMEM((1, slots), f32),
            pltpu.VMEM((2, slots), i32),
            pltpu.VMEM((1, slots), i32),
            pltpu.VMEM((4, slots), i32),
            pltpu.VMEM((2, tile, levels * half), f32),
            pltpu.VMEM((4, PIECES, members, quad // PIECES), bf16),
            pltpu.VMEM((16, PIECES, members, quad // PIECES), bf16),
            pltpu.VMEM((12, half, slots), bf16),
            pltpu.VMEM((16, half, half, slots), bf16),
            pltpu.VMEM((members, slots), f32),
            pltpu.SemaphoreType.DMA((2 * PIECES + 2,)),
            pltpu.SemaphoreType.DMA((6,)),
            pltpu.SemaphoreType.DMA((10,)),
            pltpu.SemaphoreType.REGULAR,
        ],
        compiler_params=pltpu.CompilerParams(
            collective_id=0, has_side_effects=True, vmem_limit_bytes=32 * 1024 * 1024
        ),
    )(*operands, tally)
    return out[None]


def solution(mesh):
    return jax.shard_map(
        functools.partial(on_device, mesh.shape["lat"], mesh.shape["lon"]),
        mesh=mesh,
        in_specs=(
            P(None, "lat", "lon", None),
            P(None, "lat", "lon"),
            P("lat", "lon", None, None),
            P("lat", "lon", None),
            P("lat", "lon", None, None),
            P("lat", "lon", None),
            P("lat", "lon", None, None),
            P("lat", "lon"),
        ),
        out_specs=P("lat", "lon", None),
        check_vma=False,
    )
```

```python
import functools

import jax
import jax.numpy as jnp
from jax import lax
from jax.experimental import pallas as pl
from jax.experimental.pallas import tpu as pltpu
from jax.sharding import PartitionSpec as P

MESH = pl.DeviceIdType.MESH
PIECES = 2


def kernel(
    nlat, nlon,
    dev_hbm, mis_hbm, sens_hbm, scaled_hbm, loc_hbm, cat_hbm, codes_hbm, tally,
    out_ref,
    dev, mis, sens, scaled, loc, cat, codes,
    lines, own, halo, bound, taper, acc,
    read_sem, send_sem, recv_sem, open_sem,
):
    _, levels, tile, half, members = dev.shape
    slots = sens.shape[1]
    steps = 2 * PIECES
    rows_per = half // PIECES
    quad = half * half
    p = lax.axis_index("lat")
    q = lax.axis_index("lon")
    left = lax.rem(q + nlon - 1, nlon)
    right = lax.rem(q + 1, nlon)
    has_up, has_down = p > 0, p < nlat - 1
    odd = lax.rem(p, 2)
    cross = p - 1 + 2 * odd
    has_cross = (cross >= 0) & (cross < nlat)
    has_cross_n = jnp.where(has_cross, 1, 0)
    head = q == 0
    tail = q == nlon - 1

    first = jnp.where(head | tail, 1, 0)
    halves = (first, 1 - first)
    hold = has_cross & (odd == 0)
    lead = jnp.where(has_down, 1, 0)
    lag = 1 - lead
    opening = jnp.where(hold, 0, lead)
    bands = (opening, 1 - opening)

    def has(yh):
        return (yh == 0) & has_up | (yh == 1) & has_down

    parts = [(s, r, xh, bands[r // PIECES], r % PIECES) for s, xh in enumerate(halves) for r in range(steps)]

    def columns(xh):
        return pl.ds(pl.multiple_of(xh * half, half), half)

    def local(src, dst, i):
        return pltpu.make_async_copy(src, dst, read_sem.at[i])

    weights = local(mis_hbm, mis, 0)
    reads = [
        local(
            dev_hbm.at[:, pl.ds(yh * half + c * rows_per, rows_per), columns(xh)],
            dev.at[0, :, pl.ds(r * rows_per, rows_per)],
            1 + r,
        )
        for s, r, xh, yh, c in parts[:steps]
    ]
    rest = local(dev_hbm.at[:, :, columns(halves[1])], dev.at[1], 1 + steps)
    small = [
        local(src, dst, i)
        for i, (src, dst) in enumerate(
            [(scaled_hbm, scaled), (loc_hbm, loc), (cat_hbm, cat), (codes_hbm, codes), (sens_hbm, sens)]
        )
    ]
    for copy in [weights] + reads + [rest]:
        copy.start()

    barrier = pltpu.get_barrier_semaphore()

    def signal(semaphore, row, col):
        pl.semaphore_signal(semaphore, inc=1, device_id=(row, col), device_id_type=MESH)

    pl.when(has_up)(lambda: signal(barrier, p - 1, q))
    pl.when(has_down)(lambda: signal(barrier, p + 1, q))
    signal(barrier, p, left)
    pl.when(jnp.logical_not(tail))(lambda: signal(barrier, p, right))
    pl.when((head | (odd == 1)) & has_cross)(lambda: signal(barrier, cross, left))
    pl.when(jnp.logical_not(tail) & (odd == 1) & has_cross)(lambda: signal(barrier, cross, right))
    peers = (
        jnp.minimum(p, 1) + jnp.minimum(nlat - 1 - p, 1) + jnp.where(head, 1, 2)
        + jnp.where(tail, has_cross_n, 0)
        + jnp.where(odd == 0, has_cross_n, 0) * (jnp.minimum(q, 1) + jnp.minimum(nlon - 1 - q, 1))
    )

    def enter():
        pl.semaphore_wait(barrier, peers)

        @pl.when(tail)
        def _():
            signal(open_sem, p, right)
            pl.when((odd == 1) & has_cross)(lambda: signal(open_sem, cross, right))

    soon = tail & (odd == 0)
    pl.when(soon)(enter)

    weights.wait()
    small[0].start()
    for xh in range(2):
        lines[xh] = jnp.concatenate([mis[l, :, xh * half:(xh + 1) * half] for l in range(levels)], axis=1)

    diagonal = (
        lax.rem(lax.broadcasted_iota(jnp.int32, (half, levels * half), 1), half)
        == lax.broadcasted_iota(jnp.int32, (half, levels * half), 0)
    )

    def remote(src, dst, send, recv, row, col):
        return pltpu.make_async_remote_copy(
            src_ref=src,
            dst_ref=dst,
            send_sem=send_sem.at[send],
            recv_sem=recv_sem.at[recv],
            device_id=(row, col),
            device_id_type=MESH,
        )

    def beside(yh, c, xh):
        dst = halo.at[4 * (yh + 1) + 3 * (1 - xh), c]
        return remote(own.at[2 * yh + xh, c], dst, 0, 2 + 2 * yh + 1 - xh, p, jnp.where(xh == 0, left, right))

    def across(yh, c, xh):
        return remote(own.at[2 * yh + xh, c], halo.at[12 * (1 - yh) + 1 + xh, c], 1 + yh, 1 - yh, p + 2 * yh - 1, q)

    def corner(c, xh):
        return remote(own.at[xh, c], halo.at[12 + 3 * (1 - xh), c], 3, 9 - xh, p - 1, jnp.where(xh == 0, left, right))

    def relay_copy(yh, w):
        return remote(halo.at[4 * (yh + 1) + 3 * w], halo.at[12 * (1 - yh) + 3 * w], 4 + yh, 8 - 2 * yh + w, p + 2 * yh - 1, q)

    def project(s, r, xh, yh, c):
        rows = lines[xh, pl.ds(pl.multiple_of(yh * half + c * rows_per, rows_per), rows_per), :]
        if s == 0:
            reads[r].wait()
            small[1 + r].start()
            top = r * rows_per
        else:
            if r == 0:
                rest.wait()
            top = yh * half + c * rows_per
        sums = []
        for y in range(rows_per):
            spread = jnp.where(diagonal, jnp.broadcast_to(rows[y:y + 1], diagonal.shape), 0.0)
            high = spread.astype(jnp.bfloat16)
            low = (spread - high.astype(jnp.float32)).astype(jnp.bfloat16)
            both = jnp.dot(
                jnp.concatenate([high, low], axis=0),
                dev[s, :, top + y].reshape(levels * half, members),
                preferred_element_type=jnp.float32,
            )
            sums.append(both[:half] + both[half:])
        return jnp.concatenate(sums, axis=0)

    def share(s, r, xh, yh, c, value):
        own[2 * yh + xh, c] = value.T.astype(jnp.bfloat16)
        if s == 0 and r == 0:
            pl.when(jnp.logical_not(soon))(enter)

        wrapped = head & (xh == 0)
        if r < PIECES:
            pl.when(hold & jnp.logical_not(wrapped))(corner(c, xh).start)
            pl.when(jnp.logical_not(hold | wrapped))(beside(yh, c, xh).start)
        else:
            pl.when(jnp.logical_not(wrapped))(beside(yh, c, xh).start)
        pl.when(has(yh))(across(yh, c, xh).start)
        if r == steps - 1:
            for k in range(PIECES):
                pl.when(hold & jnp.logical_not(wrapped))(beside(bands[0], k, xh).start)

    value = project(*parts[0])
    for part, following in zip(parts, parts[1:] + [None]):
        if following is not None:
            later = project(*following)
        share(*part, value)
        value = later

    for copy in small[1:4]:
        copy.wait()
    place = loc[...].astype(jnp.float32)
    radius = (tile * 0.125) * (1.0 + cat[...].astype(jnp.float32))
    radius_sq = radius * radius
    cover = codes[...]
    barred = [
        jnp.where(jnp.any(cover == code, axis=0, keepdims=True), 0.0, 4.0 * half * half)
        for code in range(9)
    ]
    for j in range(4):
        b = lax.broadcasted_iota(jnp.int32, (half, slots), 0).astype(jnp.float32) + (j - 1) * half
        gap = b - place[1:2]
        gap = gap * gap
        ds = (j + 1) // 2
        for dr in range(3):
            bound[dr * 4 + j] = (gap + barred[3 * dr + ds]).astype(jnp.bfloat16)

    row_gap = jnp.broadcast_to(place[0:1], (half, slots)).astype(jnp.bfloat16)
    reach = jnp.broadcast_to(radius_sq, (half, slots)).astype(jnp.bfloat16)
    for i in (1, 2, 0, 3):
        dr = (i + 1) // 2

        def build(y, gap):
            room = reach - gap * gap
            for j in range(4):
                t = jnp.maximum(room - bound[dr * 4 + j], jnp.bfloat16(0))
                taper[i * 4 + j, y] = t * t
            return gap - jnp.bfloat16(1)

        lax.fori_loop(0, half, build, row_gap - jnp.bfloat16((i - 1) * half), unroll=2)

    def product(slot, source):
        return jnp.dot(
            jnp.concatenate([source[c] for c in range(PIECES)], axis=1),
            taper[slot].reshape(quad, slots),
            preferred_element_type=jnp.float32,
        )

    def add(slot):
        acc[...] += product(slot, halo[slot])

    def add_band(yh):
        slot = 12 * yh + 1
        remote(own.at[pl.ds(0, 2)], halo.at[pl.ds(slot, 2)], 0, yh, p, right).wait_recv()
        for xh in range(2):
            add(slot + xh)

    def add_side(yh, w):
        add(4 * (yh + 1) + 3 * w)

    def add_corner(yh, w):
        slot = 12 * yh + 3 * w
        remote(own.at[0], halo.at[slot], 0, 6 + 2 * yh + w, p, right).wait_recv()
        add(slot)

    def relayed(yh):
        return (yh == 0) & has_up & (odd == 1) | (yh == 1) & has_down

    def relay(yh, w):
        remote(own.at[0], halo.at[4 * (yh + 1) + 3 * w], 0, 2 + 2 * yh + w, p, right).wait_recv()
        pl.when(relayed(yh))(relay_copy(yh, w).start)

    near = jnp.where(head, 1, 0)
    far = 1 - near

    @pl.when(head)
    def _():
        pl.semaphore_wait(open_sem, 1 + jnp.where(hold, 1, 0))
        for c in range(PIECES):
            pl.when(hold)(corner(c, 0).start)
        for yh in (lead, lag):
            for c in range(PIECES):
                beside(yh, c, 0).start()

    ahead = (odd == 1) & jnp.logical_not(head | tail)
    pl.when(odd == 1)(lambda: relay(lead, near))
    pl.when(ahead)(lambda: relay(lead, far))
    for yh in range(2):
        for xh in range(2):
            value = product((yh + 1) * 4 + xh + 1, own[2 * yh + xh])
            if yh == 0 and xh == 0:
                acc[...] = value
            else:
                acc[...] += value
    pl.when(has(1 - odd))(lambda: add_band(1 - odd))
    pl.when((odd == 0) & has_up)(lambda: add_band(0))
    pl.when(odd == 0)(lambda: relay(lead, near))
    relay(lag, near)
    for yh in range(2):
        add_side(yh, near)
    pl.when(jnp.logical_not(ahead))(lambda: relay(lead, far))
    pl.when(odd == 1)(lambda: relay(lag, far))
    pl.when((odd == 1) & has_down)(lambda: add_band(1))
    add_side(lead, far)
    for yh in range(2):
        pl.when(has(yh))(functools.partial(add_corner, yh, near))
    pl.when(has_down)(lambda: add_corner(1, far))
    pl.when(odd == 0)(lambda: relay(lag, far))
    add_side(lag, far)
    pl.when(has_up)(lambda: add_corner(0, far))

    small[0].wait()
    small[4].wait()
    summed = jnp.sum(acc[...] * sens[...].astype(jnp.float32), axis=0, keepdims=True)
    live = lax.broadcasted_iota(jnp.int32, (1, slots), 1) < tally[0, 0]
    value = scaled[...] * summed / ((members - 1) * radius_sq * radius_sq)
    out_ref[...] = jnp.where(live, value, 0.0)

    remote(own, halo.at[pl.ds(0, 4)], 0, 0, p, right).wait_send()

    def sent(i):
        remote(own.at[pl.ds(0, 2)], halo.at[pl.ds(0, 2)], i, 0, p, right).wait_send()

    for yh in range(2):
        pl.when(has(yh))(functools.partial(sent, 1 + yh))
        pl.when(relayed(yh))(functools.partial(sent, 4 + yh))
    pl.when(hold)(functools.partial(sent, 3))


def on_device(nlat, nlon, dev, mis, sens, scaled, loc, cat, codes, tally):
    levels, tile, _, members = dev.shape
    slots = sens.shape[3]
    half = tile // 2
    quad = half * half
    bf16, f32, i32 = jnp.bfloat16, jnp.float32, jnp.int32
    operands = [
        pltpu.with_memory_space_constraint(x, pltpu.HBM)
        for x in (dev, mis, sens[0, 0], scaled[0], loc[0, 0], cat[0], codes[0, 0])
    ]
    out = pl.pallas_call(
        functools.partial(kernel, nlat, nlon),
        out_shape=pltpu.VMEM((1, slots), f32),
        in_specs=[pl.BlockSpec(memory_space=pl.ANY)] * 7 + [pl.BlockSpec(memory_space=pltpu.SMEM)],
        out_specs=pl.BlockSpec(memory_space=pltpu.VMEM),
        scratch_shapes=[
            pltpu.VMEM((2, levels, tile, half, members), bf16),
            pltpu.VMEM((levels, tile, tile), f32),
            pltpu.VMEM((members, slots), bf16),
            pltpu.VMEM((1, slots), f32),
            pltpu.VMEM((2, slots), i32),
            pltpu.VMEM((1, slots), i32),
            pltpu.VMEM((4, slots), i32),
            pltpu.VMEM((2, tile, levels * half), f32),
            pltpu.VMEM((4, PIECES, members, quad // PIECES), bf16),
            pltpu.VMEM((16, PIECES, members, quad // PIECES), bf16),
            pltpu.VMEM((12, half, slots), bf16),
            pltpu.VMEM((16, half, half, slots), bf16),
            pltpu.VMEM((members, slots), f32),
            pltpu.SemaphoreType.DMA((2 * PIECES + 2,)),
            pltpu.SemaphoreType.DMA((6,)),
            pltpu.SemaphoreType.DMA((10,)),
            pltpu.SemaphoreType.REGULAR,
        ],
        compiler_params=pltpu.CompilerParams(
            collective_id=0, has_side_effects=True, vmem_limit_bytes=32 * 1024 * 1024
        ),
    )(*operands, tally)
    return out[None]


def solution(mesh):
    return jax.shard_map(
        functools.partial(on_device, mesh.shape["lat"], mesh.shape["lon"]),
        mesh=mesh,
        in_specs=(
            P(None, "lat", "lon", None),
            P(None, "lat", "lon"),
            P("lat", "lon", None, None),
            P("lat", "lon", None),
            P("lat", "lon", None, None),
            P("lat", "lon", None),
            P("lat", "lon", None, None),
            P("lat", "lon"),
        ),
        out_specs=P("lat", "lon", None),
        check_vma=False,
    )
```

```python
import functools

import jax
import jax.numpy as jnp
from jax import lax
from jax.experimental import pallas as pl
from jax.experimental.pallas import tpu as pltpu
from jax.sharding import PartitionSpec as P

MESH = pl.DeviceIdType.MESH
PIECES = 2


def kernel(
    nlat, nlon,
    dev_hbm, mis_hbm, sens_hbm, scaled_hbm, loc_hbm, cat_hbm, codes_hbm, tally,
    out_ref,
    dev, mis, sens, scaled, loc, cat, codes,
    lines, own, halo, bound, taper, acc,
    read_sem, send_sem, recv_sem, open_sem,
):
    _, levels, tile, half, members = dev.shape
    slots = sens.shape[1]
    steps = 2 * PIECES
    rows_per = half // PIECES
    quad = half * half
    p = lax.axis_index("lat")
    q = lax.axis_index("lon")
    left = lax.rem(q + nlon - 1, nlon)
    right = lax.rem(q + 1, nlon)
    has_up, has_down = p > 0, p < nlat - 1
    odd = lax.rem(p, 2)
    cross = p - 1 + 2 * odd
    has_cross = (cross >= 0) & (cross < nlat)
    has_cross_n = jnp.where(has_cross, 1, 0)
    head = q == 0
    tail = q == nlon - 1

    first = jnp.where(head | tail, 1, 0)
    halves = (first, 1 - first)
    hold = has_cross & (odd == 0)
    lead = jnp.where(has_down, 1, 0)
    lag = 1 - lead
    opening = jnp.where(hold, 0, lead)
    bands = (opening, 1 - opening)

    def has(yh):
        return (yh == 0) & has_up | (yh == 1) & has_down

    parts = [(s, r, xh, bands[r // PIECES], r % PIECES) for s, xh in enumerate(halves) for r in range(steps)]

    def columns(xh):
        return pl.ds(pl.multiple_of(xh * half, half), half)

    def local(src, dst, i):
        return pltpu.make_async_copy(src, dst, read_sem.at[i])

    weights = local(mis_hbm, mis, 0)
    reads = [
        local(
            dev_hbm.at[:, pl.ds(yh * half + c * rows_per, rows_per), columns(xh)],
            dev.at[0, :, pl.ds(r * rows_per, rows_per)],
            1 + r,
        )
        for s, r, xh, yh, c in parts[:steps]
    ]
    rest = [
        local(
            dev_hbm.at[:, pl.ds(yh * half, half), columns(halves[1])],
            dev.at[1, :, pl.ds(i * half, half)],
            1 + steps + i,
        )
        for i, yh in enumerate(bands)
    ]
    small = [
        local(src, dst, i)
        for i, (src, dst) in enumerate(
            [(scaled_hbm, scaled), (loc_hbm, loc), (cat_hbm, cat), (codes_hbm, codes), (sens_hbm, sens)]
        )
    ]
    for copy in [weights] + reads + rest:
        copy.start()

    barrier = pltpu.get_barrier_semaphore()

    def signal(semaphore, row, col):
        pl.semaphore_signal(semaphore, inc=1, device_id=(row, col), device_id_type=MESH)

    pl.when(has_up)(lambda: signal(barrier, p - 1, q))
    pl.when(has_down)(lambda: signal(barrier, p + 1, q))
    signal(barrier, p, left)
    pl.when(jnp.logical_not(tail))(lambda: signal(barrier, p, right))
    pl.when((head | (odd == 1)) & has_cross)(lambda: signal(barrier, cross, left))
    pl.when(jnp.logical_not(tail) & (odd == 1) & has_cross)(lambda: signal(barrier, cross, right))
    peers = (
        jnp.minimum(p, 1) + jnp.minimum(nlat - 1 - p, 1) + jnp.where(head, 1, 2)
        + jnp.where(tail, has_cross_n, 0)
        + jnp.where(odd == 0, has_cross_n, 0) * (jnp.minimum(q, 1) + jnp.minimum(nlon - 1 - q, 1))
    )

    def enter():
        pl.semaphore_wait(barrier, peers)

        @pl.when(tail)
        def _():
            signal(open_sem, p, right)
            pl.when((odd == 1) & has_cross)(lambda: signal(open_sem, cross, right))

    soon = tail & (odd == 0)
    pl.when(soon)(enter)

    weights.wait()
    small[0].start()
    for xh in range(2):
        lines[xh] = jnp.concatenate([mis[l, :, xh * half:(xh + 1) * half] for l in range(levels)], axis=1)

    diagonal = (
        lax.rem(lax.broadcasted_iota(jnp.int32, (half, levels * half), 1), half)
        == lax.broadcasted_iota(jnp.int32, (half, levels * half), 0)
    )

    def remote(src, dst, send, recv, row, col):
        return pltpu.make_async_remote_copy(
            src_ref=src,
            dst_ref=dst,
            send_sem=send_sem.at[send],
            recv_sem=recv_sem.at[recv],
            device_id=(row, col),
            device_id_type=MESH,
        )

    def beside(yh, c, xh):
        dst = halo.at[4 * (yh + 1) + 3 * (1 - xh), c]
        return remote(own.at[2 * yh + xh, c], dst, 0, 2 + 2 * yh + 1 - xh, p, jnp.where(xh == 0, left, right))

    def across(yh, c, xh):
        return remote(own.at[2 * yh + xh, c], halo.at[12 * (1 - yh) + 1 + xh, c], 1 + yh, 1 - yh, p + 2 * yh - 1, q)

    def corner(c, xh):
        return remote(own.at[xh, c], halo.at[12 + 3 * (1 - xh), c], 3, 9 - xh, p - 1, jnp.where(xh == 0, left, right))

    def relay_copy(yh, w):
        return remote(halo.at[4 * (yh + 1) + 3 * w], halo.at[12 * (1 - yh) + 3 * w], 4 + yh, 8 - 2 * yh + w, p + 2 * yh - 1, q)

    def project(s, r, xh, yh, c):
        rows = lines[xh, pl.ds(pl.multiple_of(yh * half + c * rows_per, rows_per), rows_per), :]
        if s == 0:
            reads[r].wait()
            small[1 + r].start()
            top = r * rows_per
        else:
            if c == 0:
                rest[r // PIECES].wait()
            top = r * rows_per
        high = rows.astype(jnp.bfloat16).astype(jnp.float32)
        low = rows - high
        lanes = -(-members // 128) * 128
        sums = []
        for y in range(0, rows_per, 2):
            spread = [
                jnp.where(diagonal, jnp.broadcast_to(line[k:k + 1], diagonal.shape), 0.0).astype(jnp.bfloat16)
                for k in (y, y + 1)
                for line in (high, low)
            ]
            pair = [
                jnp.pad(dev[s, :, top + k].reshape(levels * half, members), ((0, 0), (0, lanes - members)))
                for k in (y, y + 1)
            ]
            both = jnp.dot(
                jnp.concatenate(spread, axis=0),
                jnp.concatenate(pair, axis=1),
                preferred_element_type=jnp.float32,
            )
            sums.append(both[:half, :members] + both[half:2 * half, :members])
            sums.append(both[2 * half:3 * half, lanes:lanes + members] + both[3 * half:, lanes:lanes + members])
        return jnp.concatenate(sums, axis=0)

    def share(s, r, xh, yh, c, value):
        own[2 * yh + xh, c] = value.T.astype(jnp.bfloat16)
        if s == 0 and r == 0:
            pl.when(jnp.logical_not(soon))(enter)

        wrapped = head & (xh == 0)
        if r < PIECES:
            pl.when(hold & jnp.logical_not(wrapped))(corner(c, xh).start)
            pl.when(jnp.logical_not(hold | wrapped))(beside(yh, c, xh).start)
        else:
            pl.when(jnp.logical_not(wrapped))(beside(yh, c, xh).start)
        pl.when(has(yh))(across(yh, c, xh).start)
        if r == steps - 1:
            for k in range(PIECES):
                pl.when(hold & jnp.logical_not(wrapped))(beside(bands[0], k, xh).start)

    value = project(*parts[0])
    for part, following in zip(parts, parts[1:] + [None]):
        if following is not None:
            later = project(*following)
        share(*part, value)
        value = later

    for copy in small[1:4]:
        copy.wait()
    place = loc[...].astype(jnp.float32)
    radius = (tile * 0.125) * (1.0 + cat[...].astype(jnp.float32))
    radius_sq = radius * radius
    cover = codes[...]
    barred = [
        jnp.where(jnp.any(cover == code, axis=0, keepdims=True), 0.0, 4.0 * half * half)
        for code in range(9)
    ]
    for j in range(4):
        b = lax.broadcasted_iota(jnp.int32, (half, slots), 0).astype(jnp.float32) + (j - 1) * half
        gap = b - place[1:2]
        gap = gap * gap
        ds = (j + 1) // 2
        for dr in range(3):
            bound[dr * 4 + j] = (gap + barred[3 * dr + ds]).astype(jnp.bfloat16)

    row_gap = jnp.broadcast_to(place[0:1], (half, slots)).astype(jnp.bfloat16)
    reach = jnp.broadcast_to(radius_sq, (half, slots)).astype(jnp.bfloat16)
    for i in (1, 2, 0, 3):
        dr = (i + 1) // 2

        def build(y, gap):
            room = reach - gap * gap
            for j in range(4):
                t = jnp.maximum(room - bound[dr * 4 + j], jnp.bfloat16(0))
                taper[i * 4 + j, y] = t * t
            return gap - jnp.bfloat16(1)

        lax.fori_loop(0, half, build, row_gap - jnp.bfloat16((i - 1) * half), unroll=2)

    def product(slot, source):
        return jnp.dot(
            jnp.concatenate([source[c] for c in range(PIECES)], axis=1),
            taper[slot].reshape(quad, slots),
            preferred_element_type=jnp.float32,
        )

    def add(slot):
        acc[...] += product(slot, halo[slot])

    def add_band(yh):
        slot = 12 * yh + 1
        remote(own.at[pl.ds(0, 2)], halo.at[pl.ds(slot, 2)], 0, yh, p, right).wait_recv()
        for xh in range(2):
            add(slot + xh)

    def add_side(yh, w):
        add(4 * (yh + 1) + 3 * w)

    def add_corner(yh, w):
        slot = 12 * yh + 3 * w
        remote(own.at[0], halo.at[slot], 0, 6 + 2 * yh + w, p, right).wait_recv()
        add(slot)

    def relayed(yh):
        return (yh == 0) & has_up & (odd == 1) | (yh == 1) & has_down

    def relay(yh, w):
        remote(own.at[0], halo.at[4 * (yh + 1) + 3 * w], 0, 2 + 2 * yh + w, p, right).wait_recv()
        pl.when(relayed(yh))(relay_copy(yh, w).start)

    near = jnp.where(head, 1, 0)
    far = 1 - near

    @pl.when(head)
    def _():
        pl.semaphore_wait(open_sem, 1 + jnp.where(hold, 1, 0))
        for c in range(PIECES):
            pl.when(hold)(corner(c, 0).start)
        for yh in (lead, lag):
            for c in range(PIECES):
                beside(yh, c, 0).start()

    ahead = (odd == 1) & jnp.logical_not(head | tail)
    pl.when(odd == 1)(lambda: relay(lead, near))
    pl.when(ahead)(lambda: relay(lead, far))
    for yh in range(2):
        for xh in range(2):
            value = product((yh + 1) * 4 + xh + 1, own[2 * yh + xh])
            if yh == 0 and xh == 0:
                acc[...] = value
            else:
                acc[...] += value
    pl.when(has(1 - odd))(lambda: add_band(1 - odd))
    pl.when((odd == 0) & has_up)(lambda: add_band(0))
    pl.when(odd == 0)(lambda: relay(lead, near))
    relay(lag, near)
    for yh in range(2):
        add_side(yh, near)
    pl.when(jnp.logical_not(ahead))(lambda: relay(lead, far))
    pl.when(odd == 1)(lambda: relay(lag, far))
    pl.when((odd == 1) & has_down)(lambda: add_band(1))
    add_side(lead, far)
    for yh in range(2):
        pl.when(has(yh))(functools.partial(add_corner, yh, near))
    pl.when(has_down)(lambda: add_corner(1, far))
    pl.when(odd == 0)(lambda: relay(lag, far))
    add_side(lag, far)
    pl.when(has_up)(lambda: add_corner(0, far))

    small[0].wait()
    small[4].wait()
    summed = jnp.sum(acc[...] * sens[...].astype(jnp.float32), axis=0, keepdims=True)
    live = lax.broadcasted_iota(jnp.int32, (1, slots), 1) < tally[0, 0]
    value = scaled[...] * summed / ((members - 1) * radius_sq * radius_sq)
    out_ref[...] = jnp.where(live, value, 0.0)

    remote(own, halo.at[pl.ds(0, 4)], 0, 0, p, right).wait_send()

    def sent(i):
        remote(own.at[pl.ds(0, 2)], halo.at[pl.ds(0, 2)], i, 0, p, right).wait_send()

    for yh in range(2):
        pl.when(has(yh))(functools.partial(sent, 1 + yh))
        pl.when(relayed(yh))(functools.partial(sent, 4 + yh))
    pl.when(hold)(functools.partial(sent, 3))


def on_device(nlat, nlon, dev, mis, sens, scaled, loc, cat, codes, tally):
    levels, tile, _, members = dev.shape
    slots = sens.shape[3]
    half = tile // 2
    quad = half * half
    bf16, f32, i32 = jnp.bfloat16, jnp.float32, jnp.int32
    operands = [
        pltpu.with_memory_space_constraint(x, pltpu.HBM)
        for x in (dev, mis, sens[0, 0], scaled[0], loc[0, 0], cat[0], codes[0, 0])
    ]
    out = pl.pallas_call(
        functools.partial(kernel, nlat, nlon),
        out_shape=pltpu.VMEM((1, slots), f32),
        in_specs=[pl.BlockSpec(memory_space=pl.ANY)] * 7 + [pl.BlockSpec(memory_space=pltpu.SMEM)],
        out_specs=pl.BlockSpec(memory_space=pltpu.VMEM),
        scratch_shapes=[
            pltpu.VMEM((2, levels, tile, half, members), bf16),
            pltpu.VMEM((levels, tile, tile), f32),
            pltpu.VMEM((members, slots), bf16),
            pltpu.VMEM((1, slots), f32),
            pltpu.VMEM((2, slots), i32),
            pltpu.VMEM((1, slots), i32),
            pltpu.VMEM((4, slots), i32),
            pltpu.VMEM((2, tile, levels * half), f32),
            pltpu.VMEM((4, PIECES, members, quad // PIECES), bf16),
            pltpu.VMEM((16, PIECES, members, quad // PIECES), bf16),
            pltpu.VMEM((12, half, slots), bf16),
            pltpu.VMEM((16, half, half, slots), bf16),
            pltpu.VMEM((members, slots), f32),
            pltpu.SemaphoreType.DMA((2 * PIECES + 3,)),
            pltpu.SemaphoreType.DMA((6,)),
            pltpu.SemaphoreType.DMA((10,)),
            pltpu.SemaphoreType.REGULAR,
        ],
        compiler_params=pltpu.CompilerParams(
            collective_id=0, has_side_effects=True, vmem_limit_bytes=32 * 1024 * 1024
        ),
    )(*operands, tally)
    return out[None]


def solution(mesh):
    return jax.shard_map(
        functools.partial(on_device, mesh.shape["lat"], mesh.shape["lon"]),
        mesh=mesh,
        in_specs=(
            P(None, "lat", "lon", None),
            P(None, "lat", "lon"),
            P("lat", "lon", None, None),
            P("lat", "lon", None),
            P("lat", "lon", None, None),
            P("lat", "lon", None),
            P("lat", "lon", None, None),
            P("lat", "lon"),
        ),
        out_specs=P("lat", "lon", None),
        check_vma=False,
    )
```

```python
import functools

import jax
import jax.numpy as jnp
from jax import lax
from jax.experimental import pallas as pl
from jax.experimental.pallas import tpu as pltpu
from jax.sharding import PartitionSpec as P

MESH = pl.DeviceIdType.MESH
PIECES = 2


def kernel(
    nlat, nlon,
    dev_hbm, mis_hbm, sens_hbm, scaled_hbm, loc_hbm, cat_hbm, codes_hbm, tally,
    out_ref,
    dev, mis, sens, scaled, loc, cat, codes,
    lines, own, halo, bound, taper, acc,
    read_sem, send_sem, recv_sem, open_sem,
):
    _, levels, tile, half, members = dev.shape
    slots = sens.shape[1]
    steps = 2 * PIECES
    rows_per = half // PIECES
    quad = half * half
    p = lax.axis_index("lat")
    q = lax.axis_index("lon")
    left = lax.rem(q + nlon - 1, nlon)
    right = lax.rem(q + 1, nlon)
    has_up, has_down = p > 0, p < nlat - 1
    odd = lax.rem(p, 2)
    cross = p - 1 + 2 * odd
    has_cross = (cross >= 0) & (cross < nlat)
    has_cross_n = jnp.where(has_cross, 1, 0)
    head = q == 0
    tail = q == nlon - 1

    first = jnp.where(head | tail, 1, 0)
    halves = (first, 1 - first)
    hold = has_cross & (odd == 0)
    lead = jnp.where(has_down, 1, 0)
    lag = 1 - lead
    opening = jnp.where(hold, 0, lead)
    bands = (opening, 1 - opening)

    def has(yh):
        return (yh == 0) & has_up | (yh == 1) & has_down

    parts = [(s, r, xh, bands[r // PIECES], r % PIECES) for s, xh in enumerate(halves) for r in range(steps)]

    def columns(xh):
        return pl.ds(pl.multiple_of(xh * half, half), half)

    def local(src, dst, i):
        return pltpu.make_async_copy(src, dst, read_sem.at[i])

    weights = local(mis_hbm, mis, 0)
    reads = [
        local(
            dev_hbm.at[:, pl.ds(yh * half + c * rows_per, rows_per), columns(xh)],
            dev.at[0, :, pl.ds(r * rows_per, rows_per)],
            1 + r,
        )
        for s, r, xh, yh, c in parts[:steps]
    ]
    rest = [
        local(
            dev_hbm.at[:, pl.ds(yh * half, half), columns(halves[1])],
            dev.at[1, :, pl.ds(i * half, half)],
            1 + steps + i,
        )
        for i, yh in enumerate(bands)
    ]
    small = [
        local(src, dst, i)
        for i, (src, dst) in enumerate(
            [(scaled_hbm, scaled), (loc_hbm, loc), (cat_hbm, cat), (codes_hbm, codes), (sens_hbm, sens)]
        )
    ]
    weights.start()
    reads[0].start()

    barrier = pltpu.get_barrier_semaphore()

    def signal(semaphore, row, col):
        pl.semaphore_signal(semaphore, inc=1, device_id=(row, col), device_id_type=MESH)

    pl.when(has_up)(lambda: signal(barrier, p - 1, q))
    pl.when(has_down)(lambda: signal(barrier, p + 1, q))
    signal(barrier, p, left)
    pl.when(jnp.logical_not(tail))(lambda: signal(barrier, p, right))
    pl.when((head | (odd == 1)) & has_cross)(lambda: signal(barrier, cross, left))
    pl.when(jnp.logical_not(tail) & (odd == 1) & has_cross)(lambda: signal(barrier, cross, right))
    for copy in reads[1:] + rest:
        copy.start()
    peers = (
        jnp.minimum(p, 1) + jnp.minimum(nlat - 1 - p, 1) + jnp.where(head, 1, 2)
        + jnp.where(tail, has_cross_n, 0)
        + jnp.where(odd == 0, has_cross_n, 0) * (jnp.minimum(q, 1) + jnp.minimum(nlon - 1 - q, 1))
    )

    def enter():
        pl.semaphore_wait(barrier, peers)

        @pl.when(tail)
        def _():
            signal(open_sem, p, right)
            pl.when((odd == 1) & has_cross)(lambda: signal(open_sem, cross, right))

    soon = tail & (odd == 0)
    pl.when(soon)(enter)

    weights.wait()
    small[0].start()
    for xh in range(2):
        lines[xh] = jnp.concatenate([mis[l, :, xh * half:(xh + 1) * half] for l in range(levels)], axis=1)

    diagonal = (
        lax.rem(lax.broadcasted_iota(jnp.int32, (half, levels * half), 1), half)
        == lax.broadcasted_iota(jnp.int32, (half, levels * half), 0)
    )

    def remote(src, dst, send, recv, row, col):
        return pltpu.make_async_remote_copy(
            src_ref=src,
            dst_ref=dst,
            send_sem=send_sem.at[send],
            recv_sem=recv_sem.at[recv],
            device_id=(row, col),
            device_id_type=MESH,
        )

    def beside(yh, c, xh):
        dst = halo.at[4 * (yh + 1) + 3 * (1 - xh), c]
        return remote(own.at[2 * yh + xh, c], dst, 0, 2 + 2 * yh + 1 - xh, p, jnp.where(xh == 0, left, right))

    def across(yh, c, xh):
        return remote(own.at[2 * yh + xh, c], halo.at[12 * (1 - yh) + 1 + xh, c], 1, 1 - yh, p + 2 * yh - 1, q)

    def corner(c, xh):
        return remote(own.at[xh, c], halo.at[12 + 3 * (1 - xh), c], 2, 9 - xh, p - 1, jnp.where(xh == 0, left, right))

    def relay_copy(yh, w):
        return remote(halo.at[4 * (yh + 1) + 3 * w], halo.at[12 * (1 - yh) + 3 * w], 3, 8 - 2 * yh + w, p + 2 * yh - 1, q)

    def project(s, r, xh, yh, c):
        rows = lines[xh, pl.ds(pl.multiple_of(yh * half + c * rows_per, rows_per), rows_per), :]
        if s == 0:
            reads[r].wait()
            small[1 + r].start()
            top = r * rows_per
        else:
            if c == 0:
                rest[r // PIECES].wait()
            top = r * rows_per
        high = rows.astype(jnp.bfloat16).astype(jnp.float32)
        low = rows - high
        lanes = -(-members // 128) * 128
        sums = []
        for y in range(0, rows_per, 2):
            spread = [
                jnp.where(diagonal, jnp.broadcast_to(line[k:k + 1], diagonal.shape), 0.0).astype(jnp.bfloat16)
                for k in (y, y + 1)
                for line in (high, low)
            ]
            pair = [
                jnp.pad(dev[s, :, top + k].reshape(levels * half, members), ((0, 0), (0, lanes - members)))
                for k in (y, y + 1)
            ]
            both = jnp.dot(
                jnp.concatenate(spread, axis=0),
                jnp.concatenate(pair, axis=1),
                preferred_element_type=jnp.float32,
            )
            sums.append(both[:half, :members] + both[half:2 * half, :members])
            sums.append(both[2 * half:3 * half, lanes:lanes + members] + both[3 * half:, lanes:lanes + members])
        return jnp.concatenate(sums, axis=0)

    def share(s, r, xh, yh, c, value):
        own[2 * yh + xh, c] = value.T.astype(jnp.bfloat16)
        if s == 0 and r == 0:
            pl.when(jnp.logical_not(soon))(enter)

        wrapped = head & (xh == 0)
        if r < PIECES:
            pl.when(hold & jnp.logical_not(wrapped))(corner(c, xh).start)
            pl.when(jnp.logical_not(hold | wrapped))(beside(yh, c, xh).start)
        else:
            pl.when(jnp.logical_not(wrapped))(beside(yh, c, xh).start)
        pl.when(has(yh))(across(yh, c, xh).start)
        if r == steps - 1:
            for k in range(PIECES):
                pl.when(hold & jnp.logical_not(wrapped))(beside(bands[0], k, xh).start)

    value = project(*parts[0])
    for part, following in zip(parts, parts[1:] + [None]):
        if following is not None:
            later = project(*following)
        share(*part, value)
        value = later

    for copy in small[1:4]:
        copy.wait()
    place = loc[...].astype(jnp.float32)
    radius = (tile * 0.125) * (1.0 + cat[...].astype(jnp.float32))
    radius_sq = radius * radius
    cover = codes[...]
    barred = [
        jnp.where(jnp.any(cover == code, axis=0, keepdims=True), 0.0, 4.0 * half * half)
        for code in range(9)
    ]
    for j in range(4):
        b = lax.broadcasted_iota(jnp.int32, (half, slots), 0).astype(jnp.float32) + (j - 1) * half
        gap = b - place[1:2]
        gap = gap * gap
        ds = (j + 1) // 2
        for dr in range(3):
            bound[dr * 4 + j] = (gap + barred[3 * dr + ds]).astype(jnp.bfloat16)

    row_gap = jnp.broadcast_to(place[0:1], (half, slots)).astype(jnp.bfloat16)
    reach = jnp.broadcast_to(radius_sq, (half, slots)).astype(jnp.bfloat16)
    for i in (1, 2, 0, 3):
        dr = (i + 1) // 2

        def build(y, gap):
            room = reach - gap * gap
            for j in range(4):
                t = jnp.maximum(room - bound[dr * 4 + j], jnp.bfloat16(0))
                taper[i * 4 + j, y] = t * t
            return gap - jnp.bfloat16(1)

        lax.fori_loop(0, half, build, row_gap - jnp.bfloat16((i - 1) * half), unroll=2)

    def product(slot, source):
        return jnp.dot(
            jnp.concatenate([source[c] for c in range(PIECES)], axis=1),
            taper[slot].reshape(quad, slots),
            preferred_element_type=jnp.float32,
        )

    def add(slot):
        acc[...] += product(slot, halo[slot])

    def add_band(yh):
        slot = 12 * yh + 1
        remote(own.at[pl.ds(0, 2)], halo.at[pl.ds(slot, 2)], 0, yh, p, right).wait_recv()
        for xh in range(2):
            add(slot + xh)

    def add_side(yh, w):
        add(4 * (yh + 1) + 3 * w)

    def add_corner(yh, w):
        slot = 12 * yh + 3 * w
        remote(own.at[0], halo.at[slot], 0, 6 + 2 * yh + w, p, right).wait_recv()
        add(slot)

    def relayed(yh):
        return (yh == 0) & has_up & (odd == 1) | (yh == 1) & has_down

    def relay(yh, w):
        remote(own.at[0], halo.at[4 * (yh + 1) + 3 * w], 0, 2 + 2 * yh + w, p, right).wait_recv()
        pl.when(relayed(yh))(relay_copy(yh, w).start)

    near = jnp.where(head, 1, 0)
    far = 1 - near

    @pl.when(head)
    def _():
        pl.semaphore_wait(open_sem, 1 + jnp.where(hold, 1, 0))
        for c in range(PIECES):
            pl.when(hold)(corner(c, 0).start)
        for yh in (lead, lag):
            for c in range(PIECES):
                beside(yh, c, 0).start()

    ahead = (odd == 1) & jnp.logical_not(head | tail)
    pl.when(odd == 1)(lambda: relay(lead, near))
    pl.when(ahead)(lambda: relay(lead, far))
    for yh in range(2):
        for xh in range(2):
            value = product((yh + 1) * 4 + xh + 1, own[2 * yh + xh])
            if yh == 0 and xh == 0:
                acc[...] = value
            else:
                acc[...] += value
    pl.when(has(1 - odd))(lambda: add_band(1 - odd))
    pl.when((odd == 0) & has_up)(lambda: add_band(0))
    pl.when(odd == 0)(lambda: relay(lead, near))
    relay(lag, near)
    for yh in range(2):
        add_side(yh, near)
    def near_corners():
        for yh in range(2):
            pl.when(has(yh))(functools.partial(add_corner, yh, near))

    top_row = jnp.logical_not(has_up)
    pl.when(top_row)(near_corners)
    pl.when(jnp.logical_not(ahead))(lambda: relay(lead, far))
    pl.when(odd == 1)(lambda: relay(lag, far))
    pl.when((odd == 1) & has_down)(lambda: add_band(1))
    add_side(lead, far)
    pl.when(has_up)(near_corners)
    pl.when(has_down)(lambda: add_corner(1, far))
    pl.when(odd == 0)(lambda: relay(lag, far))
    add_side(lag, far)
    pl.when(has_up)(lambda: add_corner(0, far))

    small[0].wait()
    small[4].wait()
    summed = jnp.sum(acc[...] * sens[...].astype(jnp.float32), axis=0, keepdims=True)
    live = lax.broadcasted_iota(jnp.int32, (1, slots), 1) < tally[0, 0]
    value = scaled[...] * summed / ((members - 1) * radius_sq * radius_sq)
    out_ref[...] = jnp.where(live, value, 0.0)

    def sent(i, quads):
        remote(own.at[pl.ds(0, quads)], halo.at[pl.ds(0, quads)], i, 0, p, right).wait_send()

    sent(0, 4)
    both = has_up & has_down
    pl.when(both)(lambda: sent(1, 4))
    pl.when(jnp.logical_not(both) & (has_up | has_down))(lambda: sent(1, 2))
    pl.when(hold)(lambda: sent(2, 2))
    twice = relayed(0) & relayed(1)
    pl.when(twice)(lambda: sent(3, 4))
    pl.when(jnp.logical_not(twice) & (relayed(0) | relayed(1)))(lambda: sent(3, 2))


def on_device(nlat, nlon, dev, mis, sens, scaled, loc, cat, codes, tally):
    levels, tile, _, members = dev.shape
    slots = sens.shape[3]
    half = tile // 2
    quad = half * half
    bf16, f32, i32 = jnp.bfloat16, jnp.float32, jnp.int32
    operands = [
        pltpu.with_memory_space_constraint(x, pltpu.HBM)
        for x in (dev, mis, sens[0, 0], scaled[0], loc[0, 0], cat[0], codes[0, 0])
    ]
    out = pl.pallas_call(
        functools.partial(kernel, nlat, nlon),
        out_shape=pltpu.VMEM((1, slots), f32),
        in_specs=[pl.BlockSpec(memory_space=pl.ANY)] * 7 + [pl.BlockSpec(memory_space=pltpu.SMEM)],
        out_specs=pl.BlockSpec(memory_space=pltpu.VMEM),
        scratch_shapes=[
            pltpu.VMEM((2, levels, tile, half, members), bf16),
            pltpu.VMEM((levels, tile, tile), f32),
            pltpu.VMEM((members, slots), bf16),
            pltpu.VMEM((1, slots), f32),
            pltpu.VMEM((2, slots), i32),
            pltpu.VMEM((1, slots), i32),
            pltpu.VMEM((4, slots), i32),
            pltpu.VMEM((2, tile, levels * half), f32),
            pltpu.VMEM((4, PIECES, members, quad // PIECES), bf16),
            pltpu.VMEM((16, PIECES, members, quad // PIECES), bf16),
            pltpu.VMEM((12, half, slots), bf16),
            pltpu.VMEM((16, half, half, slots), bf16),
            pltpu.VMEM((members, slots), f32),
            pltpu.SemaphoreType.DMA((2 * PIECES + 3,)),
            pltpu.SemaphoreType.DMA((4,)),
            pltpu.SemaphoreType.DMA((10,)),
            pltpu.SemaphoreType.REGULAR,
        ],
        compiler_params=pltpu.CompilerParams(
            collective_id=0, has_side_effects=True, vmem_limit_bytes=32 * 1024 * 1024
        ),
    )(*operands, tally)
    return out[None]


def solution(mesh):
    return jax.shard_map(
        functools.partial(on_device, mesh.shape["lat"], mesh.shape["lon"]),
        mesh=mesh,
        in_specs=(
            P(None, "lat", "lon", None),
            P(None, "lat", "lon"),
            P("lat", "lon", None, None),
            P("lat", "lon", None),
            P("lat", "lon", None, None),
            P("lat", "lon", None),
            P("lat", "lon", None, None),
            P("lat", "lon"),
        ),
        out_specs=P("lat", "lon", None),
        check_vma=False,
    )
```

```python
import functools

import jax
import jax.numpy as jnp
from jax import lax
from jax.experimental import pallas as pl
from jax.experimental.pallas import tpu as pltpu
from jax.sharding import PartitionSpec as P

MESH = pl.DeviceIdType.MESH
PIECES = 2


def kernel(
    nlat, nlon,
    dev_hbm, mis_hbm, sens_hbm, scaled_hbm, loc_hbm, cat_hbm, codes_hbm, tally,
    out_ref,
    dev, mis, sens, scaled, loc, cat, codes,
    lines, own, halo, bound, taper, acc,
    read_sem, send_sem, recv_sem, open_sem,
):
    _, levels, tile, half, members = dev.shape
    slots = sens.shape[1]
    steps = 2 * PIECES
    rows_per = half // PIECES
    quad = half * half
    p = lax.axis_index("lat")
    q = lax.axis_index("lon")
    left = lax.rem(q + nlon - 1, nlon)
    right = lax.rem(q + 1, nlon)
    has_up, has_down = p > 0, p < nlat - 1
    odd = lax.rem(p, 2)
    cross = p - 1 + 2 * odd
    has_cross = (cross >= 0) & (cross < nlat)
    has_cross_n = jnp.where(has_cross, 1, 0)
    head = q == 0
    tail = q == nlon - 1

    first = jnp.where(head | tail, 1, 0)
    halves = (first, 1 - first)
    hold = has_cross & (odd == 0)
    lead = jnp.where(has_down, 1, 0)
    lag = 1 - lead
    opening = jnp.where(hold, 0, lead)
    bands = (opening, 1 - opening)

    def has(yh):
        return (yh == 0) & has_up | (yh == 1) & has_down

    parts = [(s, r, xh, bands[r // PIECES], r % PIECES) for s, xh in enumerate(halves) for r in range(steps)]

    def columns(xh):
        return pl.ds(pl.multiple_of(xh * half, half), half)

    def local(src, dst, i):
        return pltpu.make_async_copy(src, dst, read_sem.at[i])

    weights = local(mis_hbm, mis, 0)
    reads = [
        local(
            dev_hbm.at[:, pl.ds(yh * half + c * rows_per, rows_per), columns(xh)],
            dev.at[0, :, pl.ds(r * rows_per, rows_per)],
            1 + r,
        )
        for s, r, xh, yh, c in parts[:steps]
    ]
    rest = [
        local(
            dev_hbm.at[:, pl.ds(yh * half, half), columns(halves[1])],
            dev.at[1, :, pl.ds(i * half, half)],
            1 + steps + i,
        )
        for i, yh in enumerate(bands)
    ]
    small = [
        local(src, dst, i)
        for i, (src, dst) in enumerate(
            [(scaled_hbm, scaled), (loc_hbm, loc), (cat_hbm, cat), (codes_hbm, codes), (sens_hbm, sens)]
        )
    ]
    weights.start()
    reads[0].start()

    barrier = pltpu.get_barrier_semaphore()

    def signal(semaphore, row, col):
        pl.semaphore_signal(semaphore, inc=1, device_id=(row, col), device_id_type=MESH)

    pl.when(has_up)(lambda: signal(barrier, p - 1, q))
    pl.when(has_down)(lambda: signal(barrier, p + 1, q))
    signal(barrier, p, left)
    pl.when(jnp.logical_not(tail))(lambda: signal(barrier, p, right))
    pl.when((head | (odd == 1)) & has_cross)(lambda: signal(barrier, cross, left))
    pl.when(jnp.logical_not(tail) & (odd == 1) & has_cross)(lambda: signal(barrier, cross, right))
    for copy in reads[1:] + rest:
        copy.start()
    peers = (
        jnp.minimum(p, 1) + jnp.minimum(nlat - 1 - p, 1) + jnp.where(head, 1, 2)
        + jnp.where(tail, has_cross_n, 0)
        + jnp.where(odd == 0, has_cross_n, 0) * (jnp.minimum(q, 1) + jnp.minimum(nlon - 1 - q, 1))
    )

    def enter():
        pl.semaphore_wait(barrier, peers)

        @pl.when(tail)
        def _():
            signal(open_sem, p, right)
            pl.when((odd == 1) & has_cross)(lambda: signal(open_sem, cross, right))

    soon = tail & (odd == 0)
    pl.when(soon)(enter)

    weights.wait()
    small[0].start()
    for xh in range(2):
        lines[xh] = jnp.concatenate([mis[l, :, xh * half:(xh + 1) * half] for l in range(levels)], axis=1)

    diagonal = (
        lax.rem(lax.broadcasted_iota(jnp.int32, (half, levels * half), 1), half)
        == lax.broadcasted_iota(jnp.int32, (half, levels * half), 0)
    )

    def remote(src, dst, send, recv, row, col):
        return pltpu.make_async_remote_copy(
            src_ref=src,
            dst_ref=dst,
            send_sem=send_sem.at[send],
            recv_sem=recv_sem.at[recv],
            device_id=(row, col),
            device_id_type=MESH,
        )

    def beside(yh, c, xh):
        dst = halo.at[4 * (yh + 1) + 3 * (1 - xh), c]
        return remote(own.at[2 * yh + xh, c], dst, 0, 2 + 2 * yh + 1 - xh, p, jnp.where(xh == 0, left, right))

    def across(yh, c, xh):
        return remote(own.at[2 * yh + xh, c], halo.at[12 * (1 - yh) + 1 + xh, c], 1, 1 - yh, p + 2 * yh - 1, q)

    def corner(c, xh):
        return remote(own.at[xh, c], halo.at[12 + 3 * (1 - xh), c], 2, 9 - xh, p - 1, jnp.where(xh == 0, left, right))

    def relay_copy(yh, w):
        return remote(halo.at[4 * (yh + 1) + 3 * w], halo.at[12 * (1 - yh) + 3 * w], 3, 8 - 2 * yh + w, p + 2 * yh - 1, q)

    def project(s, r, xh, yh, c):
        rows = lines[xh, pl.ds(pl.multiple_of(yh * half + c * rows_per, rows_per), rows_per), :]
        if s == 0:
            reads[r].wait()
            small[1 + r].start()
            top = r * rows_per
        else:
            if c == 0:
                rest[r // PIECES].wait()
            top = r * rows_per
        high = rows.astype(jnp.bfloat16).astype(jnp.float32)
        low = rows - high
        lanes = -(-members // 128) * 128
        sums = []
        for y in range(0, rows_per, 2):
            spread = [
                jnp.where(diagonal, jnp.broadcast_to(line[k:k + 1], diagonal.shape), 0.0).astype(jnp.bfloat16)
                for k in (y, y + 1)
                for line in (high, low)
            ]
            pair = [
                jnp.pad(dev[s, :, top + k].reshape(levels * half, members), ((0, 0), (0, lanes - members)))
                for k in (y, y + 1)
            ]
            both = jnp.dot(
                jnp.concatenate(spread, axis=0),
                jnp.concatenate(pair, axis=1),
                preferred_element_type=jnp.float32,
            )
            sums.append(both[:half, :members] + both[half:2 * half, :members])
            sums.append(both[2 * half:3 * half, lanes:lanes + members] + both[3 * half:, lanes:lanes + members])
        return jnp.concatenate(sums, axis=0)

    def share(s, r, xh, yh, c, value):
        own[2 * yh + xh, c] = value.T.astype(jnp.bfloat16)
        if s == 0 and r == 0:
            pl.when(jnp.logical_not(soon))(enter)

        wrapped = head & (xh == 0)
        if r < PIECES:
            pl.when(hold & jnp.logical_not(wrapped))(corner(c, xh).start)
            pl.when(jnp.logical_not(hold | wrapped))(beside(yh, c, xh).start)
        else:
            pl.when(jnp.logical_not(wrapped))(beside(yh, c, xh).start)
        pl.when(has(yh))(across(yh, c, xh).start)
        if r == steps - 1:
            for k in range(PIECES):
                pl.when(hold & jnp.logical_not(wrapped))(beside(bands[0], k, xh).start)

    value = project(*parts[0])
    for part, following in zip(parts, parts[1:] + [None]):
        if following is not None:
            later = project(*following)
        share(*part, value)
        value = later

    for copy in small[1:4]:
        copy.wait()
    place = loc[...].astype(jnp.float32)
    radius = (tile * 0.125) * (1.0 + cat[...].astype(jnp.float32))
    radius_sq = radius * radius
    cover = codes[...]
    barred = [
        jnp.where(jnp.any(cover == code, axis=0, keepdims=True), 0.0, 4.0 * half * half)
        for code in range(9)
    ]
    for j in range(4):
        b = lax.broadcasted_iota(jnp.int32, (half, slots), 0).astype(jnp.float32) + (j - 1) * half
        gap = b - place[1:2]
        gap = gap * gap
        ds = (j + 1) // 2
        for dr in range(3):
            bound[dr * 4 + j] = (gap + barred[3 * dr + ds]).astype(jnp.bfloat16)

    row_gap = jnp.broadcast_to(place[0:1], (half, slots)).astype(jnp.bfloat16)
    reach = jnp.broadcast_to(radius_sq, (half, slots)).astype(jnp.bfloat16)
    for i in (1, 2, 0, 3):
        dr = (i + 1) // 2

        def build(y, gap):
            room = reach - gap * gap
            for j in range(4):
                t = jnp.maximum(room - bound[dr * 4 + j], jnp.bfloat16(0))
                taper[i * 4 + j, y] = t * t
            return gap - jnp.bfloat16(1)

        lax.fori_loop(0, half, build, row_gap - jnp.bfloat16((i - 1) * half), unroll=2)

    def product(slot, source):
        return jnp.dot(
            jnp.concatenate([source[c] for c in range(PIECES)], axis=1),
            taper[slot].reshape(quad, slots),
            preferred_element_type=jnp.float32,
        )

    def add(slot):
        acc[...] += product(slot, halo[slot])

    def add_band(yh):
        slot = 12 * yh + 1
        remote(own.at[pl.ds(0, 2)], halo.at[pl.ds(slot, 2)], 0, yh, p, right).wait_recv()
        for xh in range(2):
            add(slot + xh)

    def add_side(yh, w):
        add(4 * (yh + 1) + 3 * w)

    def add_corner(yh, w):
        slot = 12 * yh + 3 * w
        remote(own.at[0], halo.at[slot], 0, 6 + 2 * yh + w, p, right).wait_recv()
        add(slot)

    def relayed(yh):
        return (yh == 0) & has_up & (odd == 1) | (yh == 1) & has_down

    def relay(yh, w):
        remote(own.at[0], halo.at[4 * (yh + 1) + 3 * w], 0, 2 + 2 * yh + w, p, right).wait_recv()
        pl.when(relayed(yh))(relay_copy(yh, w).start)

    near = jnp.where(head, 1, 0)
    far = 1 - near

    @pl.when(head)
    def _():
        pl.semaphore_wait(open_sem, 1 + jnp.where(hold, 1, 0))
        for c in range(PIECES):
            pl.when(hold)(corner(c, 0).start)
        for yh in (lead, lag):
            for c in range(PIECES):
                beside(yh, c, 0).start()

    ahead = (odd == 1) & jnp.logical_not(head | tail)
    pl.when(odd == 1)(lambda: relay(lead, near))
    pl.when(ahead)(lambda: relay(lead, far))
    for yh in range(2):
        for xh in range(2):
            value = product((yh + 1) * 4 + xh + 1, own[2 * yh + xh])
            if yh == 0 and xh == 0:
                acc[...] = value
            else:
                acc[...] += value
    pl.when(has(1 - odd))(lambda: add_band(1 - odd))
    pl.when((odd == 0) & has_up)(lambda: add_band(0))
    pl.when(odd == 0)(lambda: relay(lead, near))
    relay(lag, near)
    for yh in range(2):
        add_side(yh, near)
    def near_corners():
        for yh in range(2):
            pl.when(has(yh))(functools.partial(add_corner, yh, near))

    top_row = jnp.logical_not(has_up)
    pl.when(top_row)(near_corners)
    pl.when(jnp.logical_not(ahead))(lambda: relay(lead, far))
    pl.when(odd == 1)(lambda: relay(lag, far))
    pl.when((odd == 1) & has_down)(lambda: add_band(1))
    add_side(lead, far)
    pl.when(has_up)(near_corners)
    pl.when(has_down)(lambda: add_corner(1, far))
    pl.when(odd == 0)(lambda: relay(lag, far))
    add_side(lag, far)
    small[0].wait()
    small[4].wait()

    def finish(total):
        summed = jnp.sum(total * sens[...].astype(jnp.float32), axis=0, keepdims=True)
        live = lax.broadcasted_iota(jnp.int32, (1, slots), 1) < tally[0, 0]
        value = scaled[...] * summed / ((members - 1) * radius_sq * radius_sq)
        out_ref[...] = jnp.where(live, value, 0.0)

    @pl.when(has_up)
    def _():
        slot = 3 * far
        remote(own.at[0], halo.at[slot], 0, 6 + far, p, right).wait_recv()
        finish(acc[...] + product(slot, halo[slot]))

    pl.when(top_row)(lambda: finish(acc[...]))

    def sent(i, quads):
        remote(own.at[pl.ds(0, quads)], halo.at[pl.ds(0, quads)], i, 0, p, right).wait_send()

    sent(0, 4)
    both = has_up & has_down
    pl.when(both)(lambda: sent(1, 4))
    pl.when(jnp.logical_not(both) & (has_up | has_down))(lambda: sent(1, 2))
    pl.when(hold)(lambda: sent(2, 2))
    twice = relayed(0) & relayed(1)
    pl.when(twice)(lambda: sent(3, 4))
    pl.when(jnp.logical_not(twice) & (relayed(0) | relayed(1)))(lambda: sent(3, 2))


def on_device(nlat, nlon, dev, mis, sens, scaled, loc, cat, codes, tally):
    levels, tile, _, members = dev.shape
    slots = sens.shape[3]
    half = tile // 2
    quad = half * half
    bf16, f32, i32 = jnp.bfloat16, jnp.float32, jnp.int32
    operands = [
        pltpu.with_memory_space_constraint(x, pltpu.HBM)
        for x in (dev, mis, sens[0, 0], scaled[0], loc[0, 0], cat[0], codes[0, 0])
    ]
    out = pl.pallas_call(
        functools.partial(kernel, nlat, nlon),
        out_shape=pltpu.VMEM((1, slots), f32),
        in_specs=[pl.BlockSpec(memory_space=pl.ANY)] * 7 + [pl.BlockSpec(memory_space=pltpu.SMEM)],
        out_specs=pl.BlockSpec(memory_space=pltpu.VMEM),
        scratch_shapes=[
            pltpu.VMEM((2, levels, tile, half, members), bf16),
            pltpu.VMEM((levels, tile, tile), f32),
            pltpu.VMEM((members, slots), bf16),
            pltpu.VMEM((1, slots), f32),
            pltpu.VMEM((2, slots), i32),
            pltpu.VMEM((1, slots), i32),
            pltpu.VMEM((4, slots), i32),
            pltpu.VMEM((2, tile, levels * half), f32),
            pltpu.VMEM((4, PIECES, members, quad // PIECES), bf16),
            pltpu.VMEM((16, PIECES, members, quad // PIECES), bf16),
            pltpu.VMEM((12, half, slots), bf16),
            pltpu.VMEM((16, half, half, slots), bf16),
            pltpu.VMEM((members, slots), f32),
            pltpu.SemaphoreType.DMA((2 * PIECES + 3,)),
            pltpu.SemaphoreType.DMA((4,)),
            pltpu.SemaphoreType.DMA((10,)),
            pltpu.SemaphoreType.REGULAR,
        ],
        compiler_params=pltpu.CompilerParams(
            collective_id=0, has_side_effects=True, vmem_limit_bytes=32 * 1024 * 1024
        ),
    )(*operands, tally)
    return out[None]


def solution(mesh):
    return jax.shard_map(
        functools.partial(on_device, mesh.shape["lat"], mesh.shape["lon"]),
        mesh=mesh,
        in_specs=(
            P(None, "lat", "lon", None),
            P(None, "lat", "lon"),
            P("lat", "lon", None, None),
            P("lat", "lon", None),
            P("lat", "lon", None, None),
            P("lat", "lon", None),
            P("lat", "lon", None, None),
            P("lat", "lon"),
        ),
        out_specs=P("lat", "lon", None),
        check_vma=False,
    )
```

```python
import functools

import jax
import jax.numpy as jnp
from jax import lax
from jax.experimental import pallas as pl
from jax.experimental.pallas import tpu as pltpu
from jax.sharding import PartitionSpec as P

MESH = pl.DeviceIdType.MESH
PIECES = 2


def kernel(
    nlat, nlon,
    dev_hbm, mis_hbm, sens_hbm, scaled_hbm, loc_hbm, cat_hbm, codes_hbm, tally,
    out_ref,
    dev, mis, sens, scaled, loc, cat, codes,
    lines, own, halo, bound, taper, acc,
    read_sem, send_sem, recv_sem, open_sem,
):
    _, levels, tile, half, members = dev.shape
    slots = sens.shape[1]
    steps = 2 * PIECES
    rows_per = half // PIECES
    quad = half * half
    p = lax.axis_index("lat")
    q = lax.axis_index("lon")
    left = lax.rem(q + nlon - 1, nlon)
    right = lax.rem(q + 1, nlon)
    has_up, has_down = p > 0, p < nlat - 1
    odd = lax.rem(p, 2)
    cross = p - 1 + 2 * odd
    has_cross = (cross >= 0) & (cross < nlat)
    has_cross_n = jnp.where(has_cross, 1, 0)
    head = q == 0
    tail = q == nlon - 1

    first = jnp.where(head | tail, 1, 0)
    halves = (first, 1 - first)
    hold = has_cross & (odd == 0)
    lead = jnp.where(has_down, 1, 0)
    lag = 1 - lead
    opening = jnp.where(hold, 0, lead)
    bands = (opening, 1 - opening)

    def has(yh):
        return (yh == 0) & has_up | (yh == 1) & has_down

    parts = [(s, r, xh, bands[r // PIECES], r % PIECES) for s, xh in enumerate(halves) for r in range(steps)]

    def columns(xh):
        return pl.ds(pl.multiple_of(xh * half, half), half)

    def local(src, dst, i):
        return pltpu.make_async_copy(src, dst, read_sem.at[i])

    weights = local(mis_hbm, mis, 0)
    reads = [
        local(
            dev_hbm.at[:, pl.ds(yh * half + c * rows_per, rows_per), columns(xh)],
            dev.at[0, :, pl.ds(r * rows_per, rows_per)],
            1 + r,
        )
        for s, r, xh, yh, c in parts[:steps]
    ]
    rest = [
        local(
            dev_hbm.at[:, pl.ds(yh * half, half), columns(halves[1])],
            dev.at[1, :, pl.ds(i * half, half)],
            1 + steps + i,
        )
        for i, yh in enumerate(bands)
    ]
    small = [
        local(src, dst, i)
        for i, (src, dst) in enumerate(
            [(scaled_hbm, scaled), (loc_hbm, loc), (cat_hbm, cat), (codes_hbm, codes), (sens_hbm, sens)]
        )
    ]
    weights.start()
    reads[0].start()

    barrier = pltpu.get_barrier_semaphore()

    def signal(semaphore, row, col):
        pl.semaphore_signal(semaphore, inc=1, device_id=(row, col), device_id_type=MESH)

    pl.when(has_up)(lambda: signal(barrier, p - 1, q))
    pl.when(has_down)(lambda: signal(barrier, p + 1, q))
    signal(barrier, p, left)
    pl.when(jnp.logical_not(tail))(lambda: signal(barrier, p, right))
    pl.when((head | (odd == 1)) & has_cross)(lambda: signal(barrier, cross, left))
    pl.when(jnp.logical_not(tail) & (odd == 1) & has_cross)(lambda: signal(barrier, cross, right))
    for copy in reads[1:] + rest:
        copy.start()
    peers = (
        jnp.minimum(p, 1) + jnp.minimum(nlat - 1 - p, 1) + jnp.where(head, 1, 2)
        + jnp.where(tail, has_cross_n, 0)
        + jnp.where(odd == 0, has_cross_n, 0) * (jnp.minimum(q, 1) + jnp.minimum(nlon - 1 - q, 1))
    )

    def enter():
        pl.semaphore_wait(barrier, peers)

        @pl.when(tail)
        def _():
            signal(open_sem, p, right)
            pl.when((odd == 1) & has_cross)(lambda: signal(open_sem, cross, right))

    soon = tail & (odd == 0)
    pl.when(soon)(enter)

    weights.wait()
    small[0].start()
    for xh in range(2):
        lines[xh] = jnp.concatenate([mis[l, :, xh * half:(xh + 1) * half] for l in range(levels)], axis=1)

    diagonal = (
        lax.rem(lax.broadcasted_iota(jnp.int32, (half, levels * half), 1), half)
        == lax.broadcasted_iota(jnp.int32, (half, levels * half), 0)
    )

    def remote(src, dst, send, recv, row, col):
        return pltpu.make_async_remote_copy(
            src_ref=src,
            dst_ref=dst,
            send_sem=send_sem.at[send],
            recv_sem=recv_sem.at[recv],
            device_id=(row, col),
            device_id_type=MESH,
        )

    def beside(yh, c, xh):
        dst = halo.at[4 * (yh + 1) + 3 * (1 - xh), c]
        return remote(own.at[2 * yh + xh, c], dst, 0, 2 + 2 * yh + 1 - xh, p, jnp.where(xh == 0, left, right))

    def across(yh, c, xh):
        return remote(own.at[2 * yh + xh, c], halo.at[12 * (1 - yh) + 1 + xh, c], 1, 1 - yh, p + 2 * yh - 1, q)

    def corner(c, xh):
        return remote(own.at[xh, c], halo.at[12 + 3 * (1 - xh), c], 2, 9 - xh, p - 1, jnp.where(xh == 0, left, right))

    def relay_copy(yh, w):
        return remote(halo.at[4 * (yh + 1) + 3 * w], halo.at[12 * (1 - yh) + 3 * w], 3, 8 - 2 * yh + w, p + 2 * yh - 1, q)

    def project(s, r, xh, yh, c):
        rows = lines[xh, pl.ds(pl.multiple_of(yh * half + c * rows_per, rows_per), rows_per), :]
        if s == 0:
            reads[r].wait()
            small[1 + r].start()
            top = r * rows_per
        else:
            if c == 0:
                rest[r // PIECES].wait()
            top = r * rows_per
        high = rows.astype(jnp.bfloat16).astype(jnp.float32)
        low = rows - high
        lanes = -(-members // 128) * 128
        sums = []
        for y in range(0, rows_per, 2):
            spread = [
                jnp.where(diagonal, jnp.broadcast_to(line[k:k + 1], diagonal.shape), 0.0).astype(jnp.bfloat16)
                for k in (y, y + 1)
                for line in (high, low)
            ]
            pair = [
                jnp.pad(dev[s, :, top + k].reshape(levels * half, members), ((0, 0), (0, lanes - members)))
                for k in (y, y + 1)
            ]
            both = jnp.dot(
                jnp.concatenate(spread, axis=0),
                jnp.concatenate(pair, axis=1),
                preferred_element_type=jnp.float32,
            )
            sums.append(both[:half, :members] + both[half:2 * half, :members])
            sums.append(both[2 * half:3 * half, lanes:lanes + members] + both[3 * half:, lanes:lanes + members])
        return jnp.concatenate(sums, axis=0)

    def share(s, r, xh, yh, c, value):
        own[2 * yh + xh, c] = value.T.astype(jnp.bfloat16)
        if s == 0 and r == 0:
            pl.when(jnp.logical_not(soon))(enter)

        wrapped = head & (xh == 0)
        if r < PIECES:
            pl.when(hold & jnp.logical_not(wrapped))(corner(c, xh).start)
            pl.when(jnp.logical_not(hold | wrapped))(beside(yh, c, xh).start)
        else:
            pl.when(jnp.logical_not(wrapped))(beside(yh, c, xh).start)
        pl.when(has(yh))(across(yh, c, xh).start)
        if r == steps - 1:
            for k in range(PIECES):
                pl.when(hold & jnp.logical_not(wrapped))(beside(bands[0], k, xh).start)

    value = project(*parts[0])
    for part, following in zip(parts, parts[1:] + [None]):
        if following is not None:
            later = project(*following)
        share(*part, value)
        value = later

    for copy in small[1:4]:
        copy.wait()
    place = loc[...].astype(jnp.float32)
    radius = (tile * 0.125) * (1.0 + cat[...].astype(jnp.float32))
    radius_sq = radius * radius
    cover = codes[...]
    barred = [
        jnp.where(jnp.any(cover == code, axis=0, keepdims=True), 0.0, 4.0 * half * half)
        for code in range(9)
    ]
    for j in range(4):
        b = lax.broadcasted_iota(jnp.int32, (half, slots), 0).astype(jnp.float32) + (j - 1) * half
        gap = b - place[1:2]
        gap = gap * gap
        ds = (j + 1) // 2
        for dr in range(3):
            bound[dr * 4 + j] = (gap + barred[3 * dr + ds]).astype(jnp.bfloat16)

    row_gap = jnp.broadcast_to(place[0:1], (half, slots)).astype(jnp.bfloat16)
    reach = jnp.broadcast_to(radius_sq, (half, slots)).astype(jnp.bfloat16)
    for i in (1, 2, 0, 3):
        dr = (i + 1) // 2

        def build(y, gap):
            room = reach - gap * gap
            for j in range(4):
                t = jnp.maximum(room - bound[dr * 4 + j], jnp.bfloat16(0))
                taper[i * 4 + j, y] = t * t
            return gap - jnp.bfloat16(1)

        lax.fori_loop(0, half, build, row_gap - jnp.bfloat16((i - 1) * half), unroll=2)

    def product(slot, source):
        return jnp.dot(
            jnp.concatenate([source[c] for c in range(PIECES)], axis=1),
            taper[slot].reshape(quad, slots),
            preferred_element_type=jnp.float32,
        )

    def add(slot):
        acc[...] += product(slot, halo[slot])

    def add_band(yh):
        slot = 12 * yh + 1
        remote(own.at[pl.ds(0, 2)], halo.at[pl.ds(slot, 2)], 0, yh, p, right).wait_recv()
        for xh in range(2):
            add(slot + xh)

    def add_side(yh, w):
        add(4 * (yh + 1) + 3 * w)

    def add_corner(yh, w):
        slot = 12 * yh + 3 * w
        remote(own.at[0], halo.at[slot], 0, 6 + 2 * yh + w, p, right).wait_recv()
        add(slot)

    def relayed(yh):
        return (yh == 0) & has_up & (odd == 1) | (yh == 1) & has_down

    def relay(yh, w):
        remote(own.at[0], halo.at[4 * (yh + 1) + 3 * w], 0, 2 + 2 * yh + w, p, right).wait_recv()
        pl.when(relayed(yh))(relay_copy(yh, w).start)

    near = jnp.where(head, 1, 0)
    far = 1 - near

    @pl.when(head)
    def _():
        pl.semaphore_wait(open_sem, 1 + jnp.where(hold, 1, 0))
        for c in range(PIECES):
            pl.when(hold)(corner(c, 0).start)
        for yh in (lead, lag):
            for c in range(PIECES):
                beside(yh, c, 0).start()

    ahead = (odd == 1) & jnp.logical_not(head | tail)
    pl.when(odd == 1)(lambda: relay(lead, near))
    pl.when(ahead)(lambda: relay(lead, far))
    for yh in range(2):
        for xh in range(2):
            value = product((yh + 1) * 4 + xh + 1, own[2 * yh + xh])
            if yh == 0 and xh == 0:
                acc[...] = value
            else:
                acc[...] += value
    pl.when(has(1 - odd))(lambda: add_band(1 - odd))
    pl.when((odd == 0) & has_up)(lambda: add_band(0))
    pl.when(odd == 0)(lambda: relay(lead, near))
    relay(lag, near)
    for yh in range(2):
        add_side(yh, near)
    def near_corners():
        for yh in range(2):
            pl.when(has(yh))(functools.partial(add_corner, yh, near))

    top_row = jnp.logical_not(has_up)
    pl.when(top_row)(near_corners)
    pl.when(jnp.logical_not(ahead))(lambda: relay(lead, far))
    pl.when((odd == 1) & has_down)(lambda: add_band(1))
    add_side(lead, far)
    pl.when(odd == 1)(lambda: relay(lag, far))
    pl.when(has_up)(near_corners)
    pl.when(has_down)(lambda: add_corner(1, far))
    pl.when(odd == 0)(lambda: relay(lag, far))
    add_side(lag, far)
    small[0].wait()
    small[4].wait()

    def finish(total):
        summed = jnp.sum(total * sens[...].astype(jnp.float32), axis=0, keepdims=True)
        live = lax.broadcasted_iota(jnp.int32, (1, slots), 1) < tally[0, 0]
        value = scaled[...] * summed / ((members - 1) * radius_sq * radius_sq)
        out_ref[...] = jnp.where(live, value, 0.0)

    @pl.when(has_up)
    def _():
        slot = 3 * far
        remote(own.at[0], halo.at[slot], 0, 6 + far, p, right).wait_recv()
        finish(acc[...] + product(slot, halo[slot]))

    pl.when(top_row)(lambda: finish(acc[...]))

    def sent(i, quads):
        remote(own.at[pl.ds(0, quads)], halo.at[pl.ds(0, quads)], i, 0, p, right).wait_send()

    sent(0, 4)
    both = has_up & has_down
    pl.when(both)(lambda: sent(1, 4))
    pl.when(jnp.logical_not(both) & (has_up | has_down))(lambda: sent(1, 2))
    pl.when(hold)(lambda: sent(2, 2))
    twice = relayed(0) & relayed(1)
    pl.when(twice)(lambda: sent(3, 4))
    pl.when(jnp.logical_not(twice) & (relayed(0) | relayed(1)))(lambda: sent(3, 2))


def on_device(nlat, nlon, dev, mis, sens, scaled, loc, cat, codes, tally):
    levels, tile, _, members = dev.shape
    slots = sens.shape[3]
    half = tile // 2
    quad = half * half
    bf16, f32, i32 = jnp.bfloat16, jnp.float32, jnp.int32
    operands = [
        pltpu.with_memory_space_constraint(x, pltpu.HBM)
        for x in (dev, mis, sens[0, 0], scaled[0], loc[0, 0], cat[0], codes[0, 0])
    ]
    out = pl.pallas_call(
        functools.partial(kernel, nlat, nlon),
        out_shape=pltpu.VMEM((1, slots), f32),
        in_specs=[pl.BlockSpec(memory_space=pl.ANY)] * 7 + [pl.BlockSpec(memory_space=pltpu.SMEM)],
        out_specs=pl.BlockSpec(memory_space=pltpu.VMEM),
        scratch_shapes=[
            pltpu.VMEM((2, levels, tile, half, members), bf16),
            pltpu.VMEM((levels, tile, tile), f32),
            pltpu.VMEM((members, slots), bf16),
            pltpu.VMEM((1, slots), f32),
            pltpu.VMEM((2, slots), i32),
            pltpu.VMEM((1, slots), i32),
            pltpu.VMEM((4, slots), i32),
            pltpu.VMEM((2, tile, levels * half), f32),
            pltpu.VMEM((4, PIECES, members, quad // PIECES), bf16),
            pltpu.VMEM((16, PIECES, members, quad // PIECES), bf16),
            pltpu.VMEM((12, half, slots), bf16),
            pltpu.VMEM((16, half, half, slots), bf16),
            pltpu.VMEM((members, slots), f32),
            pltpu.SemaphoreType.DMA((2 * PIECES + 3,)),
            pltpu.SemaphoreType.DMA((4,)),
            pltpu.SemaphoreType.DMA((10,)),
            pltpu.SemaphoreType.REGULAR,
        ],
        compiler_params=pltpu.CompilerParams(
            collective_id=0, has_side_effects=True, vmem_limit_bytes=32 * 1024 * 1024
        ),
    )(*operands, tally)
    return out[None]


def solution(mesh):
    return jax.shard_map(
        functools.partial(on_device, mesh.shape["lat"], mesh.shape["lon"]),
        mesh=mesh,
        in_specs=(
            P(None, "lat", "lon", None),
            P(None, "lat", "lon"),
            P("lat", "lon", None, None),
            P("lat", "lon", None),
            P("lat", "lon", None, None),
            P("lat", "lon", None),
            P("lat", "lon", None, None),
            P("lat", "lon"),
        ),
        out_specs=P("lat", "lon", None),
        check_vma=False,
    )
```
